32 devices in a mesh: ctx: 16 (over z, y, core), head: 2 (over x).
Axes of the slice: x: 2, y: 2, z: 4, core: 2. Of those that a mesh axis runs over, the one named last changes fastest.
Arguments:
- queries: bfloat16 [4096, 2048], P(('ctx', 'head')), may hold values from -200 to 200
- keys: bfloat16 [4096, 256], P(('ctx', 'head')), may hold values from -7 to 7
- values: bfloat16 [4096, 256], P(('ctx', 'head')), may hold values from -6 to 6
- output_cotangent: bfloat16 [4096, 2048], P(('ctx', 'head')), may hold values from -6 to 6
- doc_ids: int32 [4096], replicated, may hold values from 0 to 3, never falling along the last dimension, each value on 1 to 2048 neighbouring positions
Outputs:
- grad_queries: bfloat16 [4096, 2048], P(('ctx', 'head'))
- key_gradients: bfloat16 [4096, 256], P(('ctx', 'head'))
- value_gradients: bfloat16 [4096, 256], P(('ctx', 'head'))
The draws below stay inside these ranges and needn't reach their ends.
Inputs may be any that keep to these rules, and one draw needn't show every extreme that they name: `doc_ids`: document numbers never fall along the tokens; every number occurs; each document has 1 to 2048 tokens and one has exactly 2048.
All inputs are finite; a program needn't handle non-finite values.
Results may differ from the reference program's by a relative error of at most 0.017.
Values may be sent and summed in bfloat16 or wider, within the bound.
A program may use at most 128 MiB of HBM per device.

```python
import math
import jax
import jax.numpy as jnp
import numpy as np
from jax import lax

HEAD_DIMENSION = 128
QUERY_GROUP = 8
TOK_DEV = 256
MOST_DOC = 2048
KEY_VALUE_HEADS = 2
HQ = 16
TOTAL_TOKENS = 4096
DOCS = 4
SPAN = 8


def drawn_keys(key):
    key_initial = jnp.clip(jax.random.normal(jax.random.fold_in(key, 101), (TOTAL_TOKENS, KEY_VALUE_HEADS * HEAD_DIMENSION), jnp.float32), -6.0, 6.0)
    return key_initial


def draw_keys(key, part):
    key_initial = drawn_keys(key)
    return key_initial.astype(jnp.bfloat16)


def draw_queries(key, part):
    unmasked_rows = jnp.clip(jax.random.normal(jax.random.fold_in(key, 105), (TOTAL_TOKENS, KEY_VALUE_HEADS, QUERY_GROUP, HEAD_DIMENSION), jnp.float32), -6.0, 6.0)
    return unmasked_rows.reshape(TOTAL_TOKENS, HQ * HEAD_DIMENSION).astype(jnp.bfloat16)


def levels(stream_key, extent, pieces, least, top_value):
    def one(dim, parts):
        steps = jax.random.uniform(jax.random.fold_in(jax.random.fold_in(stream_key, 6), dim), (parts,), jnp.float32, least / len(pieces), top_value / len(pieces))
        return jnp.repeat(jnp.exp(steps), extent[dim] // parts).reshape((-1,) + (1,) * (len(extent) - dim - 1))

    factor_of = one(*pieces[0])
    for cut in pieces[1:]:
        factor_of = factor_of * one(*cut)
    return factor_of


def split_up(amount, total, limit, lean):
    portions = [(1 << 20) // math.isqrt(grade ** lean) + 1 for grade in range(2, amount + 1)]
    rest, counts = total - limit - (amount - 1), [1] * (amount - 1)
    while rest > 0:
        candidates = [i for i in range(amount - 1) if counts[i] < limit]
        whole, budget = sum([portions[i] for i in candidates]), rest
        for i in candidates:
            extra = min(limit - counts[i], max(1, budget * portions[i] // whole), rest)
            counts[i] = counts[i] + extra
            rest = rest - extra
    return np.array([limit] + counts)


def ragged(stream_key, count, total, bound, slope):
    if count == 2:
        one = jax.random.randint(stream_key, (), max(1, total - bound), min(bound, total - 1) + 1)
        return jnp.stack([one, total - one])
    lengths = jnp.asarray(split_up(count, total, bound, slope), jnp.int32)
    twos = (count - 1) // 2
    donor, sink = lengths[1:1 + 2 * twos:2], lengths[2:2 + 2 * twos:2]
    margin = jnp.minimum(donor - 1, bound - sink)
    moved = jax.random.randint(jax.random.fold_in(stream_key, 1), (twos,), 0, 1 << 20) % (margin + 1)
    lengths = lengths.at[1:1 + 2 * twos:2].set(donor - moved).at[2:2 + 2 * twos:2].set(sink + moved)
    return lengths[jax.random.permutation(jax.random.fold_in(stream_key, 2), count)]


def bell_draw(key, shape, scale, limit, split=(), kind=jnp.bfloat16):
    array = scale * jax.random.normal(key, shape, jnp.float32)
    if split:
        array = array * levels(key, shape, split, -0.22, 0.18)
    return jnp.clip(array, -limit, limit).astype(kind)


def setup_inputs(seed: int = 0) -> dict:
    arg_keys = jax.random.split(jax.random.key(seed), 6)
    return {
        "queries": draw_queries(jax.random.fold_in(arg_keys[5], 71), 0),
        "keys": draw_keys(jax.random.fold_in(arg_keys[5], 71), 0),
        "values": bell_draw(arg_keys[2], (TOTAL_TOKENS, KEY_VALUE_HEADS * HEAD_DIMENSION), 1.0, 6.0, ((0, 32),)),
        "output_cotangent": bell_draw(arg_keys[3], (TOTAL_TOKENS, HQ * HEAD_DIMENSION), 1.0, 6.0, ((0, 32),)),
        "doc_ids": jnp.searchsorted(jnp.cumsum(ragged(arg_keys[4], DOCS, TOTAL_TOKENS, MOST_DOC, 2)), jnp.arange(TOTAL_TOKENS), side="right").astype(jnp.int32),
    }


masked_score = -1.0e30


def reference(queries, keys, values, output_cotangent, doc_ids):
    scaling = HEAD_DIMENSION ** -0.5
    error_tolerance = SPAN * TOK_DEV
    window_len = error_tolerance + TOK_DEV
    query_entire = queries.reshape(TOTAL_TOKENS, KEY_VALUE_HEADS, QUERY_GROUP, HEAD_DIMENSION)
    gradient_total = output_cotangent.reshape(TOTAL_TOKENS, KEY_VALUE_HEADS, QUERY_GROUP, HEAD_DIMENSION)
    padded_key = jnp.concatenate([jnp.zeros((error_tolerance, KEY_VALUE_HEADS, HEAD_DIMENSION), keys.dtype), keys.reshape(TOTAL_TOKENS, KEY_VALUE_HEADS, HEAD_DIMENSION)], axis=0)
    padded_value = jnp.concatenate([jnp.zeros((error_tolerance, KEY_VALUE_HEADS, HEAD_DIMENSION), values.dtype), values.reshape(TOTAL_TOKENS, KEY_VALUE_HEADS, HEAD_DIMENSION)], axis=0)
    doc_all = doc_ids.astype(jnp.int32)
    doc_pad = jnp.concatenate([jnp.full((error_tolerance,), -1, jnp.int32), doc_all], axis=0)

    def one_block(carried, block_index):
        gradient_key, gradient_value = carried
        first_row = (block_index * TOK_DEV).astype(jnp.int32)
        query_blk = lax.dynamic_slice_in_dim(query_entire, first_row, TOK_DEV, 0).astype(jnp.float32)
        grad_blk = lax.dynamic_slice_in_dim(gradient_total, first_row, TOK_DEV, 0).astype(jnp.float32)
        key_blk = lax.dynamic_slice_in_dim(padded_key, first_row, window_len, 0).astype(jnp.float32)
        value_blk = lax.dynamic_slice_in_dim(padded_value, first_row, window_len, 0).astype(jnp.float32)
        query_docs = lax.dynamic_slice_in_dim(doc_all, first_row, TOK_DEV, 0)
        key_docs = lax.dynamic_slice_in_dim(doc_pad, first_row, window_len, 0)
        query_pos = jnp.arange(TOK_DEV, dtype=jnp.int32)[:, None] + error_tolerance
        key_pos = jnp.arange(window_len, dtype=jnp.int32)[None, :]
        allowed = (query_docs[:, None] == key_docs[None, :]) & (key_pos <= query_pos)
        scores = jnp.einsum("qhgd,khd->hgqk", query_blk, key_blk) * scaling
        masked = jnp.where(allowed, scores, masked_score)
        row_max = jnp.max(masked, axis=3)
        log_norm = row_max + jnp.log(jnp.sum(jnp.exp(masked - row_max[..., None]), axis=3))
        weights = jnp.where(allowed, jnp.exp(scores - log_norm[..., None]), 0.0)
        rounded = lax.optimization_barrier(weights.astype(jnp.bfloat16)).astype(jnp.float32)
        attn_out = jnp.einsum("hgqk,khd->qhgd", rounded, value_blk)
        row_dot = jnp.einsum("qhgd,qhgd->hgq", grad_blk, attn_out)
        grad_weights = jnp.einsum("qhgd,khd->hgqk", grad_blk, value_blk)
        grad_scores = (weights * (grad_weights - row_dot[..., None])).astype(jnp.bfloat16)
        grad_scores = lax.optimization_barrier(grad_scores).astype(jnp.float32)
        query_grad = jnp.einsum("hgqk,khd->qhgd", grad_scores, key_blk) * scaling
        key_part = jnp.einsum("hgqk,qhgd->khd", grad_scores, query_blk) * scaling
        value_part = jnp.einsum("hgqk,qhgd->khd", rounded, grad_blk)
        gradient_key = lax.dynamic_update_slice_in_dim(
            gradient_key, lax.dynamic_slice_in_dim(gradient_key, first_row, window_len, 0) + key_part, first_row, 0)
        gradient_value = lax.dynamic_update_slice_in_dim(
            gradient_value, lax.dynamic_slice_in_dim(gradient_value, first_row, window_len, 0) + value_part, first_row, 0)
        return (gradient_key, gradient_value), query_grad.astype(jnp.bfloat16)

    blank_gradient = jnp.zeros((error_tolerance + TOTAL_TOKENS, KEY_VALUE_HEADS, HEAD_DIMENSION), jnp.float32)
    (gradient_key, gradient_value), query_grads = lax.scan(
        one_block, (blank_gradient, blank_gradient), jnp.arange(TOTAL_TOKENS // TOK_DEV, dtype=jnp.int32))
    grad_queries = query_grads.reshape(TOTAL_TOKENS, HQ * HEAD_DIMENSION)
    key_gradients = gradient_key[error_tolerance:].astype(jnp.bfloat16).reshape(TOTAL_TOKENS, KEY_VALUE_HEADS * HEAD_DIMENSION)
    value_gradients = gradient_value[error_tolerance:].astype(jnp.bfloat16).reshape(TOTAL_TOKENS, KEY_VALUE_HEADS * HEAD_DIMENSION)
    return (grad_queries, key_gradients, value_gradients)
```

```python
import functools
import math

import jax
import jax.numpy as jnp
from jax import lax
from jax.experimental import pallas as pl
from jax.experimental.pallas import tpu as pltpu
from jax.sharding import PartitionSpec as P

SPAN = 8
PLANE = SPAN // 2
SLOTS = SPAN + PLANE

masked_score = -1e30
LOG2E = math.log2(math.e)
VMEM_LIMIT = 56 * 1024 * 1024
MESH = pl.DeviceIdType.MESH


def greet(partners):
    barrier = pltpu.get_barrier_semaphore()
    for partner in partners:
        pl.semaphore_signal(barrier, inc=1, device_id=partner, device_id_type=MESH)
    pl.semaphore_wait(barrier, len(partners))


def places():
    ctx, head = lax.axis_index("ctx"), lax.axis_index("head")
    count = lax.axis_size("ctx")
    slot = lax.rem(ctx, PLANE)
    base = ctx - slot
    up = lax.rem(ctx + PLANE, count)
    down = lax.rem(ctx + count - PLANE, count)
    far = lax.rem(slot + PLANE // 2, PLANE)
    near = slot + 1 - 2 * lax.rem(slot, 2)
    diagonal = lax.rem(near + PLANE // 2, PLANE)
    return ctx, head, slot, base, up, down, near, far, diagonal


def head_peers(head):
    count = lax.axis_size("head")
    return [lax.rem(head + step, count) for step in range(1, count)]


def rows_of(index, length):
    return pl.ds(pl.multiple_of(index * length, length), length)


def fold(x, op):
    return op(x.reshape(-1, 8, x.shape[-1]), axis=0)


def attention_kernel(
    query_in, grad_in, key_in, value_in, doc_ref, dq_out, dk_out, dv_out,
    query_ref, grad_ref, key_ref, value_ref, bias_ref, key_t_ref,
    score_ref, product_ref, weight_ref, slope_ref, query_rows, grad_rows, dq_ref,
    part_k, part_v, near_buf, own_sum, far_sum, far_buf, down_src, down_buf, final,
    local_sems, x_send, x_recv, q_send, q_recv, c_send, c_recv,
    dq_local, dq_send, dq_recv, r_send, r_recv, f_local, f_send, f_recv, *, scaling
):
    ctx, head, slot, base, up, down, near, far, diagonal = places()
    peers = head_peers(head)
    tokens = key_in.shape[0]
    length = tokens * lax.axis_size("head")
    plane = ctx // PLANE
    last = lax.axis_size("ctx") // PLANE - 1
    low, not_low = slot < PLANE // 2, slot >= PLANE // 2
    even, not_even = lax.rem(slot, 2) == 0, lax.rem(slot, 2) == 1
    pairs = [
        (key_in, key_ref, slot + SPAN),
        (value_in, value_ref, slot + SPAN),
        (query_in, query_ref, 0),
        (grad_in, grad_ref, 0),
    ]
    greet(
        [{"head": peer} for peer in peers]
        + [{"ctx": up}, {"ctx": down}, {"ctx": base + near}, {"ctx": base + far}]
    )
    x_copies = []
    for index, (source, target, block) in enumerate(pairs):
        width = target.shape[1]
        start = pl.multiple_of(block * length + head * tokens, tokens)
        copies = []
        for step, peer in enumerate(peers if index < 2 else []):
            copy = pltpu.make_async_remote_copy(
                src_ref=source.at[:, rows_of(peer, width)],
                dst_ref=target.at[pl.ds(start, tokens), :],
                send_sem=x_send.at[index, step],
                recv_sem=x_recv.at[index, step],
                device_id={"head": peer},
                device_id_type=MESH,
            )
            copy.start()
            copies.append(copy)
        local = pltpu.make_async_copy(
            source.at[:, rows_of(head, width)], target.at[pl.ds(start, tokens), :], local_sems.at[index]
        )
        local.start()
        x_copies.append((local, copies))

    width = key_ref.shape[1]
    group_size = query_ref.shape[1] // width
    rows_here = pl.ds(pl.multiple_of(head * tokens, tokens), tokens)

    def head_copies(g):
        copies = []
        for array, (source, target) in enumerate(((query_in, query_ref), (grad_in, grad_ref))):
            for step, peer in enumerate(peers):
                columns = pl.ds(pl.multiple_of((peer * group_size + g) * width, width), width)
                copies.append(
                    pltpu.make_async_remote_copy(
                        src_ref=source.at[:, columns],
                        dst_ref=target.at[rows_here, pl.ds(pl.multiple_of(g * width, width), width)],
                        send_sem=q_send.at[array, step, g],
                        recv_sem=q_recv.at[array, step, g],
                        device_id={"head": peer},
                        device_id_type=MESH,
                    )
                )
        return copies

    @pl.loop(0, group_size)
    def _(g):
        for copy in head_copies(g):
            copy.start()

    order = [head] + [lax.rem(head + len(peers) + 1 - step, len(peers) + 1) for step in range(1, len(peers) + 1)]
    pieces = range(len(order))

    def sends(kind, level):
        if level == 1:
            return True
        return ((not_low, low), (not_even, even), (low, not_low))[kind - 1][0 if level == 2 else 1]

    def receives(kind, level):
        if level == 1:
            return True
        return ((low, not_low), (even, not_even), (low, not_low))[kind - 1][0 if level == 2 else 1]

    def only(condition, body):
        if condition is True:
            body()
        else:
            pl.when(condition)(body)

    def copy_of(array, piece, kind, level):
        target = (key_ref, value_ref)[array]
        block, shift, partner = (
            (slot, 1, up), (slot, 0, base + far), (slot, 0, base + near), (far, 0, base + near)
        )[kind]
        offset = block * length + order[piece] * tokens
        source = pl.ds(pl.multiple_of((2 - level) * PLANE * length + offset, tokens), tokens)
        landing = pl.ds(pl.multiple_of((2 - level - shift) * PLANE * length + offset, tokens), tokens)
        return pltpu.make_async_remote_copy(
            src_ref=target.at[source, :],
            dst_ref=target.at[landing, :],
            send_sem=c_send.at[array, piece, kind, level],
            recv_sem=c_recv.at[array, piece, kind, level],
            device_id={"ctx": partner},
            device_id_type=MESH,
        )

    def spread(array, piece, level):
        if level < 2:
            only(plane < last, lambda: copy_of(array, piece, 0, level).start())
        only(sends(1, level), lambda: copy_of(array, piece, 1, level).start())
        only(sends(2, level), lambda: copy_of(array, piece, 2, level).start())

    def relay(piece, level):
        def body():
            for array in range(2):
                copy_of(array, piece, 1, level).wait_recv()
                copy_of(array, piece, 3, level).start()
        only(receives(1, level), body)

    for piece in pieces:
        for array in range(2):
            if piece == 0:
                x_copies[array][0].wait()
            else:
                x_copies[array][1][piece - 1].wait_recv()
            spread(array, piece, 0)
    window = bias_ref.shape[0]
    own_block = ctx
    first_key = (own_block - SPAN) * length
    lanes = doc_ref.shape[1]
    own_row = own_block * (length // lanes)
    query_docs = jnp.concatenate(
        [doc_ref[pl.ds(own_row + i, 1), :] for i in range(length // lanes)], axis=1
    )
    query_pos = own_block * length + lax.broadcasted_iota(jnp.int32, (lanes, length), 1)
    for i in range(window // lanes):
        row = jnp.maximum((own_block - SPAN) * (length // lanes) + i, 0)
        key_docs = jnp.broadcast_to(doc_ref[pl.ds(row, 1), :], (lanes, lanes)).T
        key_docs = jnp.concatenate([key_docs] * (length // lanes), axis=1)
        key_pos = first_key + i * lanes + lax.broadcasted_iota(jnp.int32, (lanes, length), 0)
        allowed = (key_docs == query_docs) & (key_pos <= query_pos) & (key_pos >= 0)
        bias_ref[i * lanes : (i + 1) * lanes, :] = jnp.where(allowed, 0.0, masked_score)
    for level in (1, 2):
        @pl.when(plane < level)
        def _():
            absent = pl.ds((2 - level) * PLANE * length, PLANE * length)
            key_ref[absent, :] = jnp.zeros((PLANE * length, width), key_ref.dtype)
            value_ref[absent, :] = jnp.zeros((PLANE * length, width), value_ref.dtype)
    for level in (1, 2):
        for piece in pieces:
            @pl.when(plane >= level)
            def _():
                for array in range(2):
                    copy_of(array, piece, 0, level - 1).wait_recv()
                    spread(array, piece, level)

            only(True if level == 1 else plane >= 1, lambda: relay(piece, level - 1))

    @pl.when(plane >= 2)
    def _():
        for piece in pieces:
            relay(piece, 2)

    for level in range(3):
        @pl.when(plane >= level)
        def _():
            for kind in (2, 3):
                def body():
                    for piece in pieces:
                        for array in range(2):
                            copy_of(array, piece, kind, level).wait_recv()
                only(receives(kind, level), body)

    for index in (2, 3):
        x_copies[index][0].wait()
    tile = length
    blocks = window // tile
    key_t_ref[...] = key_ref[pl.ds(pl.multiple_of(slot * length, length), window), :].T
    contract_last = (((1,), (1,)), ((), ()))

    def dq_copies(g):
        columns = pl.ds(pl.multiple_of(g * width, width), width)
        landing = pl.ds(pl.multiple_of((head * group_size + g) * width, width), width)
        local = pltpu.make_async_copy(dq_ref.at[rows_here, columns], dq_out.at[:, landing], dq_local.at[g])
        return [local] + [
            pltpu.make_async_remote_copy(
                src_ref=dq_ref.at[rows_of(peer, tokens), columns],
                dst_ref=dq_out.at[:, landing],
                send_sem=dq_send.at[step, g],
                recv_sem=dq_recv.at[step, g],
                device_id={"head": peer},
                device_id_type=MESH,
            )
            for step, peer in enumerate(peers)
        ]

    def query_gradient(g, inverse):
        slopes = slope_ref[:, pl.ds(pl.multiple_of(g * length, length), length)]
        dq_t = jnp.dot(key_t_ref[...], slopes, preferred_element_type=jnp.float32)
        dq_ref[:, pl.ds(pl.multiple_of(g * width, width), width)] = (dq_t * (inverse * scaling)).T.astype(jnp.bfloat16)

    def one_head(g, before):
        for copy in head_copies(g):
            copy.wait_recv()
        columns = pl.ds(pl.multiple_of(g * width, width), width)
        places_g = pl.ds(pl.multiple_of(g * length, length), length)
        query = query_ref[:, columns]
        grad = grad_ref[:, columns]
        query_gradient(jnp.maximum(g - 1, 0), before)
        top = None
        for j in range(blocks):
            here = slice(j * tile, (j + 1) * tile)
            there = pl.ds(pl.multiple_of(slot * length + j * tile, tile), tile)
            scores = lax.dot_general(key_ref[there, :], query, contract_last, preferred_element_type=jnp.float32)
            scores = scores * (scaling * LOG2E) + bias_ref[here, :]
            score_ref[here, :] = scores
            block_top = fold(scores, jnp.max)
            top = block_top if top is None else jnp.maximum(top, block_top)
        top = jnp.max(top, axis=0, keepdims=True)
        total = jnp.zeros((8, length), jnp.float32)
        dots = jnp.zeros((8, length), jnp.float32)
        for j in range(blocks):
            here = slice(j * tile, (j + 1) * tile)
            there = pl.ds(pl.multiple_of(slot * length + j * tile, tile), tile)
            powers = jnp.exp2(score_ref[here, :] - top)
            score_ref[here, :] = powers
            weight_ref[here, places_g] = powers.astype(jnp.bfloat16)
            total = total + fold(powers, jnp.sum)
            product = lax.dot_general(value_ref[there, :], grad, contract_last, preferred_element_type=jnp.float32)
            product_ref[here, :] = product
            dots = dots + fold(powers * product, jnp.sum)
        inverse = 1.0 / jnp.sum(total, axis=0, keepdims=True)
        row_dot = jnp.sum(dots, axis=0, keepdims=True) * inverse
        by_row = jnp.broadcast_to(inverse, (width, length)).T
        grad_rows[places_g, :] = (grad.astype(jnp.float32) * by_row).astype(jnp.bfloat16)
        query_rows[places_g, :] = (query.astype(jnp.float32) * by_row).astype(jnp.bfloat16)
        for j in range(blocks):
            here = slice(j * tile, (j + 1) * tile)
            slope_ref[here, places_g] = (score_ref[here, :] * (product_ref[here, :] - row_dot)).astype(jnp.bfloat16)

        @pl.when(g > 0)
        def _():
            for copy in dq_copies(g - 1):
                copy.start()

        return inverse

    inverse = lax.fori_loop(0, group_size, one_head, jnp.ones((1, length), jnp.float32))
    query_gradient(group_size - 1, inverse)
    for copy in dq_copies(group_size - 1):
        copy.start()

    parts = (part_k, part_v)
    back = peers + [head]

    def level_rows(level, position, piece):
        start = ((2 - level) * PLANE + position) * length + back[piece] * tokens
        return pl.ds(pl.multiple_of(start, tokens), tokens)

    def slab(piece):
        return pl.ds(pl.multiple_of(back[piece] * tokens, tokens), tokens)

    def sum_copy(array, piece, kind, level):
        part = parts[array]
        here = slab(piece)
        source, target, place = (
            (lambda: part.at[level_rows(level, diagonal, piece), :], lambda: near_buf.at[array, level, 0, here], {"ctx": base + near}),
            (lambda: part.at[level_rows(level, near, piece), :], lambda: near_buf.at[array, level, 1, here], {"ctx": base + near}),
            (lambda: far_sum.at[array, level, here], lambda: far_buf.at[array, level, here], {"ctx": base + far}),
            (lambda: down_src.at[array, level - 1, here], lambda: down_buf.at[array, level - 1, here], {"ctx": down}),
        )[kind]
        return pltpu.make_async_remote_copy(
            src_ref=source(),
            dst_ref=target(),
            send_sem=r_send.at[array, piece, kind, level],
            recv_sem=r_recv.at[array, piece, kind, level],
            device_id=place,
            device_id_type=MESH,
        )

    def out_of(kind, level):
        if level == 1:
            return True
        return ((low, not_low), (even, not_even), (low, not_low))[kind][0 if level == 2 else 1]

    def into(kind, level):
        if level == 1:
            return True
        return ((low, not_low), (not_even, even), (not_low, low))[kind][0 if level == 2 else 1]

    def final_copies(array, piece):
        target = (dk_out, dv_out)[array]
        source = final.at[array, slab(piece), :]
        cols = rows_of(head, width)
        if piece == len(peers):
            return pltpu.make_async_copy(source, target.at[:, cols], f_local.at[array])
        return pltpu.make_async_remote_copy(
            src_ref=source,
            dst_ref=target.at[:, cols],
            send_sem=f_send.at[array, piece],
            recv_sem=f_recv.at[array, piece],
            device_id={"head": peers[piece]},
            device_id_type=MESH,
        )

    def compute(level):
        @pl.loop((slot, PLANE, 2 * PLANE)[2 - level], (PLANE, 2 * PLANE, 2 * PLANE + 1 + slot)[2 - level])
        def _(block):
            here = pl.ds(pl.multiple_of((block - slot) * length, length), length)
            there = rows_of(block, length)
            part_k[there, :] = (
                jnp.dot(slope_ref[here, :], query_rows[...], preferred_element_type=jnp.float32) * scaling
            ).astype(jnp.bfloat16)
            part_v[there, :] = jnp.dot(
                weight_ref[here, :], grad_rows[...], preferred_element_type=jnp.float32
            ).astype(jnp.bfloat16)

        for kind in (0, 1):
            def body():
                for piece in pieces:
                    for array in range(2):
                        sum_copy(array, piece, kind, level).start()
            only(out_of(kind, level), body)

    def to_far(level):
        def body():
            for piece in pieces:
                for array in range(2):
                    here = slab(piece)
                    sum_copy(array, piece, 0, level).wait_recv()
                    far_sum[array, level, here] = (
                        parts[array][level_rows(level, far, piece), :].astype(jnp.float32)
                        + near_buf[array, level, 0, here].astype(jnp.float32)
                    ).astype(jnp.bfloat16)
                    sum_copy(array, piece, 2, level).start()
        only(into(0, level), body)

    def collect(level):
        for piece in pieces:
            for array in range(2):
                here = slab(piece)
                own_sum[array, level, here] = parts[array][level_rows(level, slot, piece), :].astype(jnp.float32)

                def add_near():
                    sum_copy(array, piece, 1, level).wait_recv()
                    own_sum[array, level, here] += near_buf[array, level, 1, here].astype(jnp.float32)
                only(into(1, level), add_near)

                def add_far():
                    sum_copy(array, piece, 2, level).wait_recv()
                    own_sum[array, level, here] += far_buf[array, level, here].astype(jnp.float32)
                only(into(2, level), add_far)

                if level < 2:
                    @pl.when(plane < last)
                    def _():
                        sum_copy(array, piece, 3, level + 1).wait_recv()
                        own_sum[array, level, here] += down_buf[array, level, here].astype(jnp.float32)

                if level > 0:
                    down_src[array, level - 1, here] = own_sum[array, level, here].astype(jnp.bfloat16)
                    sum_copy(array, piece, 3, level).start()
                else:
                    final[array, here] = own_sum[array, level, here].astype(jnp.bfloat16)
                    final_copies(array, piece).start()

    def on_level(level, body):
        only(True if level == 0 else plane >= level, lambda: body(level))

    on_level(2, compute)
    on_level(1, compute)
    on_level(2, to_far)
    on_level(0, compute)
    on_level(1, to_far)
    on_level(0, to_far)
    on_level(2, collect)
    on_level(1, collect)
    on_level(0, collect)

    for level in range(3):
        @pl.when(plane >= level)
        def _():
            for kind in range(4):
                def wait_forward():
                    for piece in pieces:
                        for array in range(2):
                            copy_of(array, piece, kind, level).wait_send()
                if kind == 0:
                    if level < 2:
                        only(plane < last, wait_forward)
                elif kind == 3:
                    only(receives(1, level), wait_forward)
                else:
                    only(sends(kind, level), wait_forward)

            for kind in range(4):
                def wait_back():
                    for piece in pieces:
                        for array in range(2):
                            sum_copy(array, piece, kind, level).wait_send()
                if kind == 3:
                    if level:
                        wait_back()
                elif kind == 2:
                    only(into(0, level), wait_back)
                else:
                    only(out_of(kind, level), wait_back)

    for _, remote in x_copies:
        for copy in remote:
            copy.wait_send()

    @pl.loop(0, group_size)
    def _(g):
        for copy in head_copies(g):
            copy.wait_send()
        for copy in dq_copies(g):
            copy.wait()

    for piece in pieces:
        for array in range(2):
            final_copies(array, piece).wait()


def attention(queries, output_cotangent, keys, values, docs):
    heads = lax.axis_size("head")
    tokens, query_width = queries.shape
    length = tokens * heads
    width = keys.shape[1] // heads
    group_size = query_width // heads // width
    window = (SPAN + 1) * length
    vmem = pl.BlockSpec(memory_space=pltpu.VMEM)
    dma = pltpu.SemaphoreType.DMA
    rows = (length, query_width // heads)
    block = (length, width)
    bf16, f32 = jnp.bfloat16, jnp.float32
    narrow = jax.ShapeDtypeStruct((tokens, width * heads), bf16)
    return pl.pallas_call(
        functools.partial(attention_kernel, scaling=width ** (-0.5)),
        out_shape=(jax.ShapeDtypeStruct((tokens, query_width), bf16), narrow, narrow),
        in_specs=[vmem] * 5,
        out_specs=(vmem,) * 3,
        scratch_shapes=[
            pltpu.VMEM(rows, bf16),
            pltpu.VMEM(rows, bf16),
            pltpu.VMEM((SLOTS * length, width), bf16),
            pltpu.VMEM((SLOTS * length, width), bf16),
            pltpu.VMEM((window, length), f32),
            pltpu.VMEM((width, window), bf16),
            pltpu.VMEM((window, length), f32),
            pltpu.VMEM((window, length), f32),
            pltpu.VMEM((window, group_size * length), bf16),
            pltpu.VMEM((window, group_size * length), bf16),
            pltpu.VMEM((group_size * length, width), bf16),
            pltpu.VMEM((group_size * length, width), bf16),
            pltpu.VMEM(rows, bf16),
            pltpu.VMEM((SLOTS * length, width), bf16),
            pltpu.VMEM((SLOTS * length, width), bf16),
            pltpu.VMEM((2, 3, 2) + block, bf16),
            pltpu.VMEM((2, 3) + block, f32),
            pltpu.VMEM((2, 3) + block, bf16),
            pltpu.VMEM((2, 3) + block, bf16),
            pltpu.VMEM((2, 2) + block, bf16),
            pltpu.VMEM((2, 2) + block, bf16),
            pltpu.VMEM((2,) + block, bf16),
            dma((4,)), dma((2, heads)), dma((2, heads)),
            dma((2, heads, group_size)), dma((2, heads, group_size)),
            dma((2, heads, 4, 3)), dma((2, heads, 4, 3)),
            dma((group_size,)), dma((heads, group_size)), dma((heads, group_size)),
            dma((2, heads, 4, 3)), dma((2, heads, 4, 3)),
            dma((2,)), dma((2, heads)), dma((2, heads)),
        ],
        compiler_params=pltpu.CompilerParams(
            collective_id=0, has_side_effects=True, vmem_limit_bytes=VMEM_LIMIT
        ),
    )(queries, output_cotangent, keys, values, docs)


def settle_kernel(dq_ref, dk_ref, dv_ref, dq_out, dk_out, dv_out, sems):
    copies = [
        pltpu.make_async_copy(source, target, sems.at[index])
        for index, (source, target) in enumerate(((dq_ref, dq_out), (dk_ref, dk_out), (dv_ref, dv_out)))
    ]
    for copy in copies:
        copy.start()
    for copy in copies:
        copy.wait()


def settle(*arrays):
    return pl.pallas_call(
        settle_kernel,
        out_shape=tuple(jax.ShapeDtypeStruct(array.shape, array.dtype) for array in arrays),
        in_specs=[pl.BlockSpec(memory_space=pltpu.VMEM)] * 3,
        out_specs=(pl.BlockSpec(memory_space=pl.ANY),) * 3,
        scratch_shapes=[pltpu.SemaphoreType.DMA((3,))],
    )(*arrays)


def on_device(queries, keys, values, output_cotangent, doc_ids):
    docs = doc_ids.reshape(-1, keys.shape[1] // lax.axis_size("head"))
    return settle(*attention(queries, output_cotangent, keys, values, docs))


def solution(mesh):
    rows = P(("ctx", "head"), None)
    return jax.shard_map(
        on_device,
        mesh=mesh,
        in_specs=(rows, rows, rows, rows, P()),
        out_specs=(rows, rows, rows),
        check_vma=False,
    )
```

```python
import functools
import math

import jax
import jax.numpy as jnp
from jax import lax
from jax.experimental import pallas as pl
from jax.experimental.pallas import tpu as pltpu
from jax.sharding import PartitionSpec as P

SPAN = 8
PLANE = SPAN // 2
SLOTS = SPAN + PLANE
EARLY = 2

masked_score = -1e30
LOG2E = math.log2(math.e)
VMEM_LIMIT = 56 * 1024 * 1024
MESH = pl.DeviceIdType.MESH


def greet(partners):
    barrier = pltpu.get_barrier_semaphore()
    for partner in partners:
        pl.semaphore_signal(barrier, inc=1, device_id=partner, device_id_type=MESH)
    pl.semaphore_wait(barrier, len(partners))


def places():
    ctx, head = lax.axis_index("ctx"), lax.axis_index("head")
    count = lax.axis_size("ctx")
    slot = lax.rem(ctx, PLANE)
    base = ctx - slot
    up = lax.rem(ctx + PLANE, count)
    down = lax.rem(ctx + count - PLANE, count)
    far = lax.rem(slot + PLANE // 2, PLANE)
    near = slot + 1 - 2 * lax.rem(slot, 2)
    diagonal = lax.rem(near + PLANE // 2, PLANE)
    return ctx, head, slot, base, up, down, near, far, diagonal


def head_peers(head):
    count = lax.axis_size("head")
    return [lax.rem(head + step, count) for step in range(1, count)]


def rows_of(index, length):
    return pl.ds(pl.multiple_of(index * length, length), length)


def fold(x, op):
    return op(x.reshape(-1, 8, x.shape[-1]), axis=0)


def attention_kernel(
    query_in, grad_in, key_in, value_in, doc_ref, dq_out, dk_out, dv_out,
    query_ref, grad_ref, key_ref, value_ref, bias_ref, key_t_ref,
    score_ref, product_ref, weight_ref, slope_ref, query_rows, grad_rows, dq_ref, stat_ref, dot_ref, factor_ref,
    part_k, part_v, near_buf, own_sum, far_sum, far_buf, down_src, down_buf, final,
    local_sems, x_send, x_recv, q_send, q_recv, c_send, c_recv,
    dq_local, dq_send, dq_recv, r_send, r_recv, f_local, f_send, f_recv, *, scaling
):
    ctx, head, slot, base, up, down, near, far, diagonal = places()
    peers = head_peers(head)
    tokens = key_in.shape[0]
    length = tokens * lax.axis_size("head")
    plane = ctx // PLANE
    last = lax.axis_size("ctx") // PLANE - 1
    low, not_low = slot < PLANE // 2, slot >= PLANE // 2
    even, not_even = lax.rem(slot, 2) == 0, lax.rem(slot, 2) == 1
    pairs = [
        (key_in, key_ref, slot + SPAN),
        (value_in, value_ref, slot + SPAN),
        (query_in, query_ref, 0),
        (grad_in, grad_ref, 0),
    ]
    greet(
        [{"head": peer} for peer in peers]
        + [{"ctx": up}, {"ctx": down}, {"ctx": base + near}, {"ctx": base + far}]
    )
    x_copies = []
    for index, (source, target, block) in enumerate(pairs):
        width = target.shape[1]
        start = pl.multiple_of(block * length + head * tokens, tokens)
        copies = []
        for step, peer in enumerate(peers if index < 2 else []):
            copy = pltpu.make_async_remote_copy(
                src_ref=source.at[:, rows_of(peer, width)],
                dst_ref=target.at[pl.ds(start, tokens), :],
                send_sem=x_send.at[index, step],
                recv_sem=x_recv.at[index, step],
                device_id={"head": peer},
                device_id_type=MESH,
            )
            copy.start()
            copies.append(copy)
        local = pltpu.make_async_copy(
            source.at[:, rows_of(head, width)], target.at[pl.ds(start, tokens), :], local_sems.at[index]
        )
        local.start()
        x_copies.append((local, copies))

    width = key_ref.shape[1]
    group_size = query_ref.shape[1] // width
    rows_here = pl.ds(pl.multiple_of(head * tokens, tokens), tokens)

    def head_copies(g):
        copies = []
        for array, (source, target) in enumerate(((query_in, query_ref), (grad_in, grad_ref))):
            for step, peer in enumerate(peers):
                columns = pl.ds(pl.multiple_of((peer * group_size + g) * width, width), width)
                copies.append(
                    pltpu.make_async_remote_copy(
                        src_ref=source.at[:, columns],
                        dst_ref=target.at[rows_here, pl.ds(pl.multiple_of(g * width, width), width)],
                        send_sem=q_send.at[array, step, g],
                        recv_sem=q_recv.at[array, step, g],
                        device_id={"head": peer},
                        device_id_type=MESH,
                    )
                )
        return copies

    @pl.loop(0, group_size)
    def _(g):
        for copy in head_copies(g):
            copy.start()

    order = [head] + [lax.rem(head + len(peers) + 1 - step, len(peers) + 1) for step in range(1, len(peers) + 1)]
    pieces = range(len(order))

    def sends(kind, level):
        if level == 1:
            return True
        return ((not_low, low), (not_even, even), (low, not_low))[kind - 1][0 if level == 2 else 1]

    def receives(kind, level):
        if level == 1:
            return True
        return ((low, not_low), (even, not_even), (low, not_low))[kind - 1][0 if level == 2 else 1]

    def only(condition, body):
        if condition is True:
            body()
        else:
            pl.when(condition)(body)

    def copy_of(array, piece, kind, level):
        target = (key_ref, value_ref)[array]
        block, shift, partner = (
            (slot, 1, up), (slot, 0, base + far), (slot, 0, base + near), (far, 0, base + near)
        )[kind]
        offset = block * length + order[piece] * tokens
        source = pl.ds(pl.multiple_of((2 - level) * PLANE * length + offset, tokens), tokens)
        landing = pl.ds(pl.multiple_of((2 - level - shift) * PLANE * length + offset, tokens), tokens)
        return pltpu.make_async_remote_copy(
            src_ref=target.at[source, :],
            dst_ref=target.at[landing, :],
            send_sem=c_send.at[array, piece, kind, level],
            recv_sem=c_recv.at[array, piece, kind, level],
            device_id={"ctx": partner},
            device_id_type=MESH,
        )

    def spread(array, piece, level):
        if level < 2:
            only(plane < last, lambda: copy_of(array, piece, 0, level).start())
        only(sends(1, level), lambda: copy_of(array, piece, 1, level).start())
        only(sends(2, level), lambda: copy_of(array, piece, 2, level).start())

    def relay(piece, level):
        def body():
            for array in range(2):
                copy_of(array, piece, 1, level).wait_recv()
                copy_of(array, piece, 3, level).start()
        only(receives(1, level), body)

    for piece in pieces:
        for array in range(2):
            if piece == 0:
                x_copies[array][0].wait()
            else:
                x_copies[array][1][piece - 1].wait_recv()
            spread(array, piece, 0)
    window = bias_ref.shape[0]
    own_block = ctx
    mixed = SPAN + 1 - PLANE
    places_of = [PLANE + i for i in range(PLANE)] + [
        slot + i + jnp.where(i >= PLANE - slot, PLANE, 0) for i in range(mixed)
    ]
    lanes = doc_ref.shape[1]
    half = PLANE * length
    own_row = own_block * (length // lanes)
    query_docs = jnp.concatenate(
        [doc_ref[pl.ds(own_row + i, 1), :] for i in range(length // lanes)], axis=1
    )
    query_pos = own_block * length + lax.broadcasted_iota(jnp.int32, (lanes, length), 1)
    for block, spot in enumerate(places_of):
        for i in range(length // lanes):
            key_block = base - SPAN + spot
            row = jnp.maximum(key_block * (length // lanes) + i, 0)
            key_docs = jnp.broadcast_to(doc_ref[pl.ds(row, 1), :], (lanes, lanes)).T
            key_docs = jnp.concatenate([key_docs] * (length // lanes), axis=1)
            key_pos = key_block * length + i * lanes + lax.broadcasted_iota(jnp.int32, (lanes, length), 0)
            allowed = (key_docs == query_docs) & (key_pos <= query_pos) & (key_pos >= 0)
            first = block * length + i * lanes
            bias_ref[first : first + lanes, :] = jnp.where(allowed, 0.0, masked_score)
    for level in (1, 2):
        @pl.when(plane < level)
        def _():
            absent = pl.ds((2 - level) * PLANE * length, PLANE * length)
            key_ref[absent, :] = jnp.zeros((PLANE * length, width), key_ref.dtype)
            value_ref[absent, :] = jnp.zeros((PLANE * length, width), value_ref.dtype)
    for level in (1, 2):
        for piece in pieces:
            @pl.when(plane >= level)
            def _():
                for array in range(2):
                    copy_of(array, piece, 0, level - 1).wait_recv()
                    spread(array, piece, level)

            only(True if level == 1 else plane >= 1, lambda: relay(piece, level - 1))

    def arrived(level):
        @pl.when(plane >= level)
        def _():
            for kind in (2, 3):
                def body():
                    for piece in pieces:
                        for array in range(2):
                            copy_of(array, piece, kind, level).wait_recv()
                only(receives(kind, level), body)

    contract_last = (((1,), (1,)), ((), ()))

    def columns_of(g, size):
        return pl.ds(pl.multiple_of(g * size, size), size)

    def softmax(g, group):
        blocks = range(PLANE) if group == 0 else range(PLANE, SPAN + 1)
        first = blocks[0] * length
        query = query_ref[:, columns_of(g, width)]
        grad = grad_ref[:, columns_of(g, width)]
        places_g = columns_of(g, length)
        top = None
        for j in blocks:
            here = slice(j * length, (j + 1) * length)
            slots = slice(j * length - first, (j + 1) * length - first)
            there = rows_of(places_of[j], length)
            scores = lax.dot_general(key_ref[there, :], query, contract_last, preferred_element_type=jnp.float32)
            scores = scores * (scaling * LOG2E) + bias_ref[here, :]
            score_ref[slots, :] = scores
            block_top = fold(scores, jnp.max)
            top = block_top if top is None else jnp.maximum(top, block_top)
        top = jnp.max(top, axis=0, keepdims=True)
        total = jnp.zeros((8, length), jnp.float32)
        dots = jnp.zeros((8, length), jnp.float32)
        for j in blocks:
            here = slice(j * length, (j + 1) * length)
            slots = slice(j * length - first, (j + 1) * length - first)
            there = rows_of(places_of[j], length)
            powers = jnp.exp2(score_ref[slots, :] - top)
            weight_ref[here, places_g] = powers.astype(jnp.bfloat16)
            total = total + fold(powers, jnp.sum)
            product = lax.dot_general(value_ref[there, :], grad, contract_last, preferred_element_type=jnp.float32)
            product_ref[here, places_g] = product
            dots = dots + fold(powers * product, jnp.sum)
        for index, value in enumerate((top, jnp.sum(total, axis=0, keepdims=True), jnp.sum(dots, axis=0, keepdims=True))):
            stat_ref[g, group, index] = jnp.broadcast_to(value, (8, length))

    def join(g):
        places_g = columns_of(g, length)
        query = query_ref[:, columns_of(g, width)].astype(jnp.float32)
        grad = grad_ref[:, columns_of(g, width)].astype(jnp.float32)
        tops = [stat_ref[g, group, 0] for group in range(2)]
        top = jnp.maximum(*tops)
        powers = [jnp.exp2(value - top) for value in tops]
        inverse = 1.0 / sum(power * stat_ref[g, group, 1] for group, power in enumerate(powers))
        dot_ref[:, places_g] = sum(power * stat_ref[g, group, 2] for group, power in enumerate(powers)) * inverse
        for group, power in enumerate(powers):
            factor = power * inverse
            factor_ref[group, :, places_g] = factor * scaling
            by_row = jnp.broadcast_to(factor[:1], (width, length)).T
            grad_rows[group, places_g, :] = (grad * by_row).astype(jnp.bfloat16)
            query_rows[group, places_g, :] = (query * by_row).astype(jnp.bfloat16)

    def head_here(g):
        for copy in head_copies(g):
            copy.wait_recv()

    for index in (2, 3):
        x_copies[index][0].wait()
    arrived(0)
    arrived(1)
    early = min(EARLY, group_size)

    @pl.loop(0, early)
    def _(g):
        head_here(g)
        softmax(g, 0)

    @pl.when(plane >= 2)
    def _():
        for piece in pieces:
            relay(piece, 2)

    arrived(2)

    @pl.loop(0, early)
    def _(g):
        softmax(g, 1)
        join(g)

    @pl.loop(early, group_size)
    def _(g):
        head_here(g)
        softmax(g, 0)
        softmax(g, 1)
        join(g)

    def dq_copies(g):
        columns = columns_of(g, width)
        landing = pl.ds(pl.multiple_of((head * group_size + g) * width, width), width)
        local = pltpu.make_async_copy(dq_ref.at[rows_here, columns], dq_out.at[:, landing], dq_local.at[g])
        return [local] + [
            pltpu.make_async_remote_copy(
                src_ref=dq_ref.at[rows_of(peer, tokens), columns],
                dst_ref=dq_out.at[:, landing],
                send_sem=dq_send.at[step, g],
                recv_sem=dq_recv.at[step, g],
                device_id={"head": peer},
                device_id_type=MESH,
            )
            for step, peer in enumerate(peers)
        ]

    def query_gradients():
        for j, spot in enumerate(places_of):
            key_t_ref[:, j * length : (j + 1) * length] = key_ref[rows_of(spot, length), :].T

        @pl.loop(0, group_size)
        def _(g):
            places_g = columns_of(g, length)
            dq_t = jnp.zeros((width, length), jnp.float32)
            for group, here in enumerate((slice(0, half), slice(half, window))):
                part = jnp.dot(key_t_ref[:, here], slope_ref[here, places_g], preferred_element_type=jnp.float32)
                dq_t = dq_t + part * factor_ref[group, :1, places_g]
            dq_ref[:, columns_of(g, width)] = dq_t.T.astype(jnp.bfloat16)
            for copy in dq_copies(g):
                copy.start()

    parts = (part_k, part_v)
    back = peers + [head]

    def level_rows(level, position, piece):
        start = ((2 - level) * PLANE + position) * length + back[piece] * tokens
        return pl.ds(pl.multiple_of(start, tokens), tokens)

    def slab(piece):
        return pl.ds(pl.multiple_of(back[piece] * tokens, tokens), tokens)

    def sum_copy(array, piece, kind, level):
        part = parts[array]
        here = slab(piece)
        source, target, place = (
            (lambda: part.at[level_rows(level, diagonal, piece), :], lambda: near_buf.at[array, level, 0, here], {"ctx": base + near}),
            (lambda: part.at[level_rows(level, near, piece), :], lambda: near_buf.at[array, level, 1, here], {"ctx": base + near}),
            (lambda: far_sum.at[array, level, here], lambda: far_buf.at[array, level, here], {"ctx": base + far}),
            (lambda: down_src.at[array, level - 1, here], lambda: down_buf.at[array, level - 1, here], {"ctx": down}),
        )[kind]
        return pltpu.make_async_remote_copy(
            src_ref=source(),
            dst_ref=target(),
            send_sem=r_send.at[array, piece, kind, level],
            recv_sem=r_recv.at[array, piece, kind, level],
            device_id=place,
            device_id_type=MESH,
        )

    def out_of(kind, level):
        if level == 1:
            return True
        return ((low, not_low), (even, not_even), (low, not_low))[kind][0 if level == 2 else 1]

    def into(kind, level):
        if level == 1:
            return True
        return ((low, not_low), (not_even, even), (not_low, low))[kind][0 if level == 2 else 1]

    def final_copies(array, piece):
        target = (dk_out, dv_out)[array]
        source = final.at[array, slab(piece), :]
        cols = rows_of(head, width)
        if piece == len(peers):
            return pltpu.make_async_copy(source, target.at[:, cols], f_local.at[array])
        return pltpu.make_async_remote_copy(
            src_ref=source,
            dst_ref=target.at[:, cols],
            send_sem=f_send.at[array, piece],
            recv_sem=f_recv.at[array, piece],
            device_id={"head": peers[piece]},
            device_id_type=MESH,
        )

    def slopes(here):
        for g in range(group_size):
            places_g = slice(g * length, (g + 1) * length)
            slope_ref[here, places_g] = (
                weight_ref[here, places_g].astype(jnp.float32)
                * (product_ref[here, places_g] - dot_ref[:1, places_g])
            ).astype(jnp.bfloat16)

    def sums(here, there, group):
        part_k[there, :] = (
            jnp.dot(slope_ref[here, :], query_rows[group], preferred_element_type=jnp.float32) * scaling
        ).astype(jnp.bfloat16)
        part_v[there, :] = jnp.dot(
            weight_ref[here, :], grad_rows[group], preferred_element_type=jnp.float32
        ).astype(jnp.bfloat16)

    def near_rows():
        @pl.loop(0, slot + 1)
        def _(i):
            slopes(rows_of(SPAN - slot + i, length))

    def compute(level):
        if level == 1:
            for i in range(PLANE):
                here = slice(i * length, (i + 1) * length)
                slopes(here)
                sums(here, slice((PLANE + i) * length, (PLANE + i + 1) * length), 0)
        elif level == 2:
            @pl.loop(0, PLANE - slot)
            def _(i):
                here = rows_of(PLANE + i, length)
                slopes(here)
                sums(here, rows_of(slot + i, length), 1)
        else:
            @pl.loop(0, slot + 1)
            def _(i):
                sums(rows_of(SPAN - slot + i, length), rows_of(2 * PLANE + i, length), 1)

        for kind in (0, 1):
            def body():
                for piece in pieces:
                    for array in range(2):
                        sum_copy(array, piece, kind, level).start()
            only(out_of(kind, level), body)

    def to_far(level):
        def body():
            for piece in pieces:
                for array in range(2):
                    here = slab(piece)
                    sum_copy(array, piece, 0, level).wait_recv()
                    far_sum[array, level, here] = (
                        parts[array][level_rows(level, far, piece), :].astype(jnp.float32)
                        + near_buf[array, level, 0, here].astype(jnp.float32)
                    ).astype(jnp.bfloat16)
                    sum_copy(array, piece, 2, level).start()
        only(into(0, level), body)

    def collect(level):
        for piece in pieces:
            for array in range(2):
                here = slab(piece)
                own_sum[array, level, here] = parts[array][level_rows(level, slot, piece), :].astype(jnp.float32)

                def add_near():
                    sum_copy(array, piece, 1, level).wait_recv()
                    own_sum[array, level, here] += near_buf[array, level, 1, here].astype(jnp.float32)
                only(into(1, level), add_near)

                def add_far():
                    sum_copy(array, piece, 2, level).wait_recv()
                    own_sum[array, level, here] += far_buf[array, level, here].astype(jnp.float32)
                only(into(2, level), add_far)

                if level < 2:
                    @pl.when(plane < last)
                    def _():
                        sum_copy(array, piece, 3, level + 1).wait_recv()
                        own_sum[array, level, here] += down_buf[array, level, here].astype(jnp.float32)

                if level > 0:
                    down_src[array, level - 1, here] = own_sum[array, level, here].astype(jnp.bfloat16)
                    sum_copy(array, piece, 3, level).start()
                else:
                    final[array, here] = own_sum[array, level, here].astype(jnp.bfloat16)
                    final_copies(array, piece).start()

    def on_level(level, body):
        only(True if level == 0 else plane >= level, lambda: body(level))

    @pl.when(plane < 1)
    def _():
        slope_ref[:half, :] = jnp.zeros((half, slope_ref.shape[1]), slope_ref.dtype)

    @pl.when(plane < 2)
    def _():
        @pl.loop(0, PLANE - slot)
        def _(i):
            slope_ref[rows_of(PLANE + i, length), :] = jnp.zeros((length, slope_ref.shape[1]), slope_ref.dtype)

    on_level(2, compute)
    on_level(1, compute)
    on_level(2, to_far)
    near_rows()
    on_level(1, to_far)
    query_gradients()
    on_level(2, collect)
    on_level(0, compute)
    on_level(0, to_far)
    on_level(1, collect)
    on_level(0, collect)

    for level in range(3):
        @pl.when(plane >= level)
        def _():
            for kind in range(4):
                def wait_forward():
                    for piece in pieces:
                        for array in range(2):
                            copy_of(array, piece, kind, level).wait_send()
                if kind == 0:
                    if level < 2:
                        only(plane < last, wait_forward)
                elif kind == 3:
                    only(receives(1, level), wait_forward)
                else:
                    only(sends(kind, level), wait_forward)

            for kind in range(4):
                def wait_back():
                    for piece in pieces:
                        for array in range(2):
                            sum_copy(array, piece, kind, level).wait_send()
                if kind == 3:
                    if level:
                        wait_back()
                elif kind == 2:
                    only(into(0, level), wait_back)
                else:
                    only(out_of(kind, level), wait_back)

    for _, remote in x_copies:
        for copy in remote:
            copy.wait_send()

    @pl.loop(0, group_size)
    def _(g):
        for copy in head_copies(g):
            copy.wait_send()
        for copy in dq_copies(g):
            copy.wait()

    for piece in pieces:
        for array in range(2):
            final_copies(array, piece).wait()


def attention(queries, output_cotangent, keys, values, docs):
    heads = lax.axis_size("head")
    tokens, query_width = queries.shape
    length = tokens * heads
    width = keys.shape[1] // heads
    group_size = query_width // heads // width
    window = (SPAN + 1) * length
    vmem = pl.BlockSpec(memory_space=pltpu.VMEM)
    anywhere = pl.BlockSpec(memory_space=pl.ANY)
    dma = pltpu.SemaphoreType.DMA
    rows = (length, query_width // heads)
    block = (length, width)
    bf16, f32 = jnp.bfloat16, jnp.float32
    narrow = jax.ShapeDtypeStruct((tokens, width * heads), bf16)
    return pl.pallas_call(
        functools.partial(attention_kernel, scaling=width ** (-0.5)),
        out_shape=(jax.ShapeDtypeStruct((tokens, query_width), bf16), narrow, narrow),
        in_specs=[anywhere] * 4 + [vmem],
        out_specs=(anywhere,) * 3,
        scratch_shapes=[
            pltpu.VMEM(rows, bf16),
            pltpu.VMEM(rows, bf16),
            pltpu.VMEM((SLOTS * length, width), bf16),
            pltpu.VMEM((SLOTS * length, width), bf16),
            pltpu.VMEM((window, length), f32),
            pltpu.VMEM((width, window), bf16),
            pltpu.VMEM((window - PLANE * length, length), f32),
            pltpu.VMEM((window, group_size * length), f32),
            pltpu.VMEM((window, group_size * length), bf16),
            pltpu.VMEM((window, group_size * length), bf16),
            pltpu.VMEM((2, group_size * length, width), bf16),
            pltpu.VMEM((2, group_size * length, width), bf16),
            pltpu.VMEM(rows, bf16),
            pltpu.VMEM((group_size, 2, 3, 8, length), f32),
            pltpu.VMEM((8, group_size * length), f32),
            pltpu.VMEM((2, 8, group_size * length), f32),
            pltpu.VMEM((SLOTS * length, width), bf16),
            pltpu.VMEM((SLOTS * length, width), bf16),
            pltpu.VMEM((2, 3, 2) + block, bf16),
            pltpu.VMEM((2, 3) + block, f32),
            pltpu.VMEM((2, 3) + block, bf16),
            pltpu.VMEM((2, 3) + block, bf16),
            pltpu.VMEM((2, 2) + block, bf16),
            pltpu.VMEM((2, 2) + block, bf16),
            pltpu.VMEM((2,) + block, bf16),
            dma((4,)), dma((2, heads)), dma((2, heads)),
            dma((2, heads, group_size)), dma((2, heads, group_size)),
            dma((2, heads, 4, 3)), dma((2, heads, 4, 3)),
            dma((group_size,)), dma((heads, group_size)), dma((heads, group_size)),
            dma((2, heads, 4, 3)), dma((2, heads, 4, 3)),
            dma((2,)), dma((2, heads)), dma((2, heads)),
        ],
        compiler_params=pltpu.CompilerParams(
            collective_id=0, has_side_effects=True, vmem_limit_bytes=VMEM_LIMIT
        ),
    )(queries, output_cotangent, keys, values, docs)


def settle_kernel(dq_ref, dk_ref, dv_ref, dq_out, dk_out, dv_out, sems):
    copies = [
        pltpu.make_async_copy(source, target, sems.at[index])
        for index, (source, target) in enumerate(((dq_ref, dq_out), (dk_ref, dk_out), (dv_ref, dv_out)))
    ]
    for copy in copies:
        copy.start()
    for copy in copies:
        copy.wait()


def settle(*arrays):
    return pl.pallas_call(
        settle_kernel,
        out_shape=tuple(jax.ShapeDtypeStruct(array.shape, array.dtype) for array in arrays),
        in_specs=[pl.BlockSpec(memory_space=pltpu.VMEM)] * 3,
        out_specs=(pl.BlockSpec(memory_space=pl.ANY),) * 3,
        scratch_shapes=[pltpu.SemaphoreType.DMA((3,))],
    )(*arrays)


def on_device(queries, keys, values, output_cotangent, doc_ids):
    docs = doc_ids.reshape(-1, keys.shape[1] // lax.axis_size("head"))
    return settle(*attention(queries, output_cotangent, keys, values, docs))


def solution(mesh):
    rows = P(("ctx", "head"), None)
    return jax.shard_map(
        on_device,
        mesh=mesh,
        in_specs=(rows, rows, rows, rows, P()),
        out_specs=(rows, rows, rows),
        check_vma=False,
    )
```

```python
import functools
import math

import jax
import jax.numpy as jnp
from jax import lax
from jax.experimental import pallas as pl
from jax.experimental.pallas import tpu as pltpu
from jax.sharding import PartitionSpec as P

SPAN = 8
PLANE = SPAN // 2
SLOTS = SPAN + PLANE
EARLY = 4
RELAY = 1

masked_score = -1e30
LOG2E = math.log2(math.e)
VMEM_LIMIT = 56 * 1024 * 1024
MESH = pl.DeviceIdType.MESH


def greet(partners):
    barrier = pltpu.get_barrier_semaphore()
    for partner in partners:
        pl.semaphore_signal(barrier, inc=1, device_id=partner, device_id_type=MESH)
    pl.semaphore_wait(barrier, len(partners))


def places():
    ctx, head = lax.axis_index("ctx"), lax.axis_index("head")
    count = lax.axis_size("ctx")
    slot = lax.rem(ctx, PLANE)
    base = ctx - slot
    up = lax.rem(ctx + PLANE, count)
    down = lax.rem(ctx + count - PLANE, count)
    far = lax.rem(slot + PLANE // 2, PLANE)
    near = slot + 1 - 2 * lax.rem(slot, 2)
    diagonal = lax.rem(near + PLANE // 2, PLANE)
    return ctx, head, slot, base, up, down, near, far, diagonal


def head_peers(head):
    count = lax.axis_size("head")
    return [lax.rem(head + step, count) for step in range(1, count)]


def rows_of(index, length):
    return pl.ds(pl.multiple_of(index * length, length), length)


def fold(x, op):
    return op(x.reshape(-1, 8, x.shape[-1]), axis=0)


def drain(ref, sem):
    pltpu.make_async_copy(ref, ref, sem).wait()


def attention_kernel(
    query_in, grad_in, key_in, value_in, doc_in, dq_out, dk_out, dv_out,
    query_ref, grad_ref, pair_ref, doc_ref, bias_ref, key_t_ref,
    score_ref, product_ref, weight_ref, slope_ref, query_rows, grad_rows, dq_ref, stat_ref, dot_ref, factor_ref,
    part_ref, near_buf, own_sum, far_sum, far_buf, down_src, down_buf, final,
    local_sems, x_send, x_recv, q_send, q_recv, c_send, c_recv, c_block,
    dq_sems, r_send, r_recv, f_sems, *, scaling
):
    ctx, head, slot, base, up, down, near, far, diagonal = places()
    peers = head_peers(head)
    tokens = key_in.shape[0]
    length = tokens * lax.axis_size("head")
    plane = ctx // PLANE
    last = lax.axis_size("ctx") // PLANE - 1
    low, not_low = slot < PLANE // 2, slot >= PLANE // 2
    even, not_even = lax.rem(slot, 2) == 0, lax.rem(slot, 2) == 1
    width = pair_ref.shape[1] // 2
    others = len(peers) * tokens
    doc_copy = pltpu.make_async_copy(doc_in, doc_ref, local_sems.at[2])
    doc_copy.start()
    greet(
        [{"head": peer} for peer in peers]
        + [{"ctx": up}, {"ctx": down}, {"ctx": base + near}, {"ctx": base + far}]
    )
    rows_here = pl.ds(pl.multiple_of(head * tokens, tokens), tokens)
    own_rows = pl.ds(pl.multiple_of((slot + SPAN) * length + head * tokens, tokens), tokens)
    lanes_of = (slice(0, width), slice(width, 2 * width))
    for array, source in enumerate((key_in, value_in)):
        pltpu.make_async_copy(
            source.at[:, rows_of(head, width)], pair_ref.at[own_rows, lanes_of[array]], local_sems.at[0]
        ).start()
        for step, peer in enumerate(peers):
            pltpu.make_async_remote_copy(
                src_ref=source.at[:, rows_of(peer, width)],
                dst_ref=pair_ref.at[own_rows, lanes_of[array]],
                send_sem=x_send,
                recv_sem=x_recv.at[step],
                device_id={"head": peer},
                device_id_type=MESH,
            ).start()
    for source, target in ((query_in, query_ref), (grad_in, grad_ref)):
        pltpu.make_async_copy(
            source.at[:, rows_of(head, target.shape[1])], target.at[rows_here, :], local_sems.at[1]
        ).start()
    group_size = query_ref.shape[1] // width

    def head_copies(g):
        copies = []
        for source, target in ((query_in, query_ref), (grad_in, grad_ref)):
            for step, peer in enumerate(peers):
                columns = pl.ds(pl.multiple_of((peer * group_size + g) * width, width), width)
                copies.append(
                    pltpu.make_async_remote_copy(
                        src_ref=source.at[:, columns],
                        dst_ref=target.at[rows_here, pl.ds(pl.multiple_of(g * width, width), width)],
                        send_sem=q_send,
                        recv_sem=q_recv.at[g],
                        device_id={"head": peer},
                        device_id_type=MESH,
                    )
                )
        return copies

    @pl.loop(0, group_size)
    def _(g):
        for copy in head_copies(g):
            copy.start()

    order = [head] + [lax.rem(head + len(peers) + 1 - step, len(peers) + 1) for step in range(1, len(peers) + 1)]
    pieces = range(len(order))

    def sends(kind, level):
        if level == 1:
            return True
        return ((not_low, low), (not_even, even), (low, not_low))[kind - 1][0 if level == 2 else 1]

    def receives(kind, level):
        if level == 1:
            return True
        return ((low, not_low), (even, not_even), (low, not_low))[kind - 1][0 if level == 2 else 1]

    def only(condition, body):
        if condition is True:
            body()
        else:
            pl.when(condition)(body)

    def copy_of(piece, kind, level):
        block, shift, partner = (
            (slot, 1, up), (slot, 0, base + far), (slot, 0, base + near), (far, 0, base + near)
        )[kind]
        offset = block * length + order[piece] * tokens
        source = pl.ds(pl.multiple_of((2 - level) * PLANE * length + offset, tokens), tokens)
        landing = pl.ds(pl.multiple_of((2 - level - shift) * PLANE * length + offset, tokens), tokens)
        return pltpu.make_async_remote_copy(
            src_ref=pair_ref.at[source, :],
            dst_ref=pair_ref.at[landing, :],
            send_sem=c_send.at[kind, level],
            recv_sem=c_recv.at[piece, kind, level] if kind < 2 else c_block.at[kind - 2, level],
            device_id={"ctx": partner},
            device_id_type=MESH,
        )

    def spread(piece, level):
        if level < 2:
            only(plane < last, lambda: copy_of(piece, 0, level).start())
        only(sends(1, level), lambda: copy_of(piece, 1, level).start())
        only(sends(2, level), lambda: copy_of(piece, 2, level).start())

    def relay(piece, level):
        def body():
            copy_of(piece, 1, level).wait_recv()
            copy_of(piece, 3, level).start()
        only(receives(1, level), body)

    whole_block = pair_ref.at[:length, :]
    for piece in pieces:
        if piece == 0:
            drain(pair_ref.at[:tokens, :], local_sems.at[0])
        else:
            drain(pair_ref.at[:tokens, :], x_recv.at[piece - 1])
        spread(piece, 0)
    doc_copy.wait()
    window = bias_ref.shape[0]
    own_block = ctx
    mixed = SPAN + 1 - PLANE
    places_of = [PLANE + i for i in range(PLANE)] + [
        slot + i + jnp.where(i >= PLANE - slot, PLANE, 0) for i in range(mixed)
    ]
    lanes = doc_ref.shape[1]
    half = PLANE * length
    own_row = own_block * (length // lanes)
    query_docs = jnp.concatenate(
        [doc_ref[pl.ds(own_row + i, 1), :] for i in range(length // lanes)], axis=1
    )
    query_pos = own_block * length + lax.broadcasted_iota(jnp.int32, (lanes, length), 1)
    for block, spot in enumerate(places_of):
        for i in range(length // lanes):
            key_block = base - SPAN + spot
            row = jnp.maximum(key_block * (length // lanes) + i, 0)
            key_docs = jnp.broadcast_to(doc_ref[pl.ds(row, 1), :], (lanes, lanes)).T
            key_docs = jnp.concatenate([key_docs] * (length // lanes), axis=1)
            key_pos = key_block * length + i * lanes + lax.broadcasted_iota(jnp.int32, (lanes, length), 0)
            allowed = (key_docs == query_docs) & (key_pos <= query_pos) & (key_pos >= 0)
            first = block * length + i * lanes
            bias_ref[first : first + lanes, :] = jnp.where(allowed, 0.0, masked_score)
    for level in (1, 2):
        @pl.when(plane < level)
        def _():
            absent = pl.ds((2 - level) * PLANE * length, PLANE * length)
            pair_ref[absent, :] = jnp.zeros((PLANE * length, 2 * width), pair_ref.dtype)
    for level in (1, 2):
        for piece in pieces:
            @pl.when(plane >= level)
            def _():
                copy_of(piece, 0, level - 1).wait_recv()
                spread(piece, level)

            only(True if level == 1 else plane >= 1, lambda: relay(piece, level - 1))

    def arrived(level):
        @pl.when(plane >= level)
        def _():
            for kind in (2, 3):
                only(receives(kind, level), lambda: drain(whole_block, c_block.at[kind - 2, level]))

    contract_last = (((1,), (1,)), ((), ()))

    def columns_of(g, size):
        return pl.ds(pl.multiple_of(g * size, size), size)

    def softmax(g, group):
        blocks = range(PLANE) if group == 0 else range(PLANE, SPAN + 1)
        first = blocks[0] * length
        query = query_ref[:, columns_of(g, width)]
        grad = grad_ref[:, columns_of(g, width)]
        places_g = columns_of(g, length)
        top = None
        for j in blocks:
            here = slice(j * length, (j + 1) * length)
            slots = slice(j * length - first, (j + 1) * length - first)
            there = rows_of(places_of[j], length)
            scores = lax.dot_general(pair_ref[there, :width], query, contract_last, preferred_element_type=jnp.float32)
            scores = scores * (scaling * LOG2E) + bias_ref[here, :]
            score_ref[slots, :] = scores
            block_top = fold(scores, jnp.max)
            top = block_top if top is None else jnp.maximum(top, block_top)
        top = jnp.max(top, axis=0, keepdims=True)
        total = jnp.zeros((8, length), jnp.float32)
        dots = jnp.zeros((8, length), jnp.float32)
        for j in blocks:
            here = slice(j * length, (j + 1) * length)
            slots = slice(j * length - first, (j + 1) * length - first)
            there = rows_of(places_of[j], length)
            powers = jnp.exp2(score_ref[slots, :] - top)
            weight_ref[here, places_g] = powers.astype(jnp.bfloat16)
            total = total + fold(powers, jnp.sum)
            product = lax.dot_general(pair_ref[there, width:], grad, contract_last, preferred_element_type=jnp.float32)
            product_ref[here, places_g] = product
            dots = dots + fold(powers * product, jnp.sum)
        for index, value in enumerate((top, jnp.sum(total, axis=0, keepdims=True), jnp.sum(dots, axis=0, keepdims=True))):
            stat_ref[g, group, index] = jnp.broadcast_to(value, (8, length))

    def join(g):
        places_g = columns_of(g, length)
        query = query_ref[:, columns_of(g, width)].astype(jnp.float32)
        grad = grad_ref[:, columns_of(g, width)].astype(jnp.float32)
        tops = [stat_ref[g, group, 0] for group in range(2)]
        top = jnp.maximum(*tops)
        powers = [jnp.exp2(value - top) for value in tops]
        inverse = 1.0 / sum(power * stat_ref[g, group, 1] for group, power in enumerate(powers))
        dot_ref[:, places_g] = sum(power * stat_ref[g, group, 2] for group, power in enumerate(powers)) * inverse
        for group, power in enumerate(powers):
            factor = power * inverse
            factor_ref[group, :, places_g] = factor * scaling
            by_row = jnp.broadcast_to(factor[:1], (width, length)).T
            grad_rows[group, places_g, :] = (grad * by_row).astype(jnp.bfloat16)
            query_rows[group, places_g, :] = (query * by_row).astype(jnp.bfloat16)

    def head_here(g):
        drain(query_rows.at[0, : 2 * others, :], q_recv.at[g])

    drain(query_ref.at[: 2 * tokens, :], local_sems.at[1])
    arrived(0)
    arrived(1)
    early = min(EARLY, group_size)

    @pl.loop(0, early)
    def _(g):
        head_here(g)
        softmax(g, 0)

        @pl.when((g == RELAY) & (plane >= 2))
        def _():
            for piece in pieces:
                relay(piece, 2)

    arrived(2)

    @pl.loop(0, early)
    def _(g):
        softmax(g, 1)
        join(g)

    @pl.loop(early, group_size)
    def _(g):
        head_here(g)
        softmax(g, 0)
        softmax(g, 1)
        join(g)

    def dq_copies(g):
        columns = columns_of(g, width)
        landing = pl.ds(pl.multiple_of((head * group_size + g) * width, width), width)
        local = pltpu.make_async_copy(dq_ref.at[rows_here, columns], dq_out.at[:, landing], dq_sems.at[0])
        return [local] + [
            pltpu.make_async_remote_copy(
                src_ref=dq_ref.at[rows_of(peer, tokens), columns],
                dst_ref=dq_out.at[:, landing],
                send_sem=dq_sems.at[1],
                recv_sem=dq_sems.at[2],
                device_id={"head": peer},
                device_id_type=MESH,
            )
            for peer in peers
        ]

    def query_gradients():
        for j, spot in enumerate(places_of):
            key_t_ref[:, j * length : (j + 1) * length] = pair_ref[rows_of(spot, length), :width].T

        @pl.loop(0, group_size)
        def _(g):
            places_g = columns_of(g, length)
            dq_t = jnp.zeros((width, length), jnp.float32)
            for group, here in enumerate((slice(0, half), slice(half, window))):
                part = jnp.dot(key_t_ref[:, here], slope_ref[here, places_g], preferred_element_type=jnp.float32)
                dq_t = dq_t + part * factor_ref[group, :1, places_g]
            dq_ref[:, columns_of(g, width)] = dq_t.T.astype(jnp.bfloat16)
            for copy in dq_copies(g):
                copy.start()

    back = peers + [head]

    def level_rows(level, position, piece):
        start = ((2 - level) * PLANE + position) * length + back[piece] * tokens
        return pl.ds(pl.multiple_of(start, tokens), tokens)

    def slab(piece):
        return pl.ds(pl.multiple_of(back[piece] * tokens, tokens), tokens)

    def sum_copy(piece, kind, level):
        here = slab(piece)
        source, target, place = (
            (lambda: part_ref.at[level_rows(level, diagonal, piece), :], lambda: near_buf.at[level, 0, here], {"ctx": base + near}),
            (lambda: part_ref.at[level_rows(level, near, piece), :], lambda: near_buf.at[level, 1, here], {"ctx": base + near}),
            (lambda: far_sum.at[level, here], lambda: far_buf.at[level, here], {"ctx": base + far}),
            (lambda: down_src.at[level - 1, here], lambda: down_buf.at[level - 1, here], {"ctx": down}),
        )[kind]
        return pltpu.make_async_remote_copy(
            src_ref=source(),
            dst_ref=target(),
            send_sem=r_send.at[kind, level],
            recv_sem=r_recv.at[piece, kind, level],
            device_id=place,
            device_id_type=MESH,
        )

    def out_of(kind, level):
        if level == 1:
            return True
        return ((low, not_low), (even, not_even), (low, not_low))[kind][0 if level == 2 else 1]

    def into(kind, level):
        if level == 1:
            return True
        return ((low, not_low), (not_even, even), (not_low, low))[kind][0 if level == 2 else 1]

    def final_copies(piece):
        copies = []
        for array, target in enumerate((dk_out, dv_out)):
            source = final.at[slab(piece), lanes_of[array]]
            cols = rows_of(head, width)
            if piece == len(peers):
                copies.append(pltpu.make_async_copy(source, target.at[:, cols], f_sems.at[0]))
            else:
                copies.append(
                    pltpu.make_async_remote_copy(
                        src_ref=source,
                        dst_ref=target.at[:, cols],
                        send_sem=f_sems.at[1],
                        recv_sem=f_sems.at[2],
                        device_id={"head": peers[piece]},
                        device_id_type=MESH,
                    )
                )
        return copies

    def slopes(here):
        for g in range(group_size):
            places_g = slice(g * length, (g + 1) * length)
            slope_ref[here, places_g] = (
                weight_ref[here, places_g].astype(jnp.float32)
                * (product_ref[here, places_g] - dot_ref[:1, places_g])
            ).astype(jnp.bfloat16)

    def sums(here, there, group):
        part_ref[there, :width] = (
            jnp.dot(slope_ref[here, :], query_rows[group], preferred_element_type=jnp.float32) * scaling
        ).astype(jnp.bfloat16)
        part_ref[there, width:] = jnp.dot(
            weight_ref[here, :], grad_rows[group], preferred_element_type=jnp.float32
        ).astype(jnp.bfloat16)

    def near_rows():
        @pl.loop(0, slot + 1)
        def _(i):
            slopes(rows_of(SPAN - slot + i, length))

    def compute(level):
        if level == 1:
            for i in range(PLANE):
                here = slice(i * length, (i + 1) * length)
                slopes(here)
                sums(here, slice((PLANE + i) * length, (PLANE + i + 1) * length), 0)
        elif level == 2:
            @pl.loop(0, PLANE - slot)
            def _(i):
                here = rows_of(PLANE + i, length)
                slopes(here)
                sums(here, rows_of(slot + i, length), 1)
        else:
            @pl.loop(0, slot + 1)
            def _(i):
                sums(rows_of(SPAN - slot + i, length), rows_of(2 * PLANE + i, length), 1)

        for kind in (0, 1):
            def body():
                for piece in pieces:
                    sum_copy(piece, kind, level).start()
            only(out_of(kind, level), body)

    def to_far(level):
        def body():
            for piece in pieces:
                here = slab(piece)
                sum_copy(piece, 0, level).wait_recv()
                far_sum[level, here] = (
                    part_ref[level_rows(level, far, piece), :].astype(jnp.float32)
                    + near_buf[level, 0, here].astype(jnp.float32)
                ).astype(jnp.bfloat16)
                sum_copy(piece, 2, level).start()
        only(into(0, level), body)

    def collect(level):
        for piece in pieces:
            here = slab(piece)
            own_sum[level, here] = part_ref[level_rows(level, slot, piece), :].astype(jnp.float32)

            def add_near():
                sum_copy(piece, 1, level).wait_recv()
                own_sum[level, here] += near_buf[level, 1, here].astype(jnp.float32)
            only(into(1, level), add_near)

            def add_far():
                sum_copy(piece, 2, level).wait_recv()
                own_sum[level, here] += far_buf[level, here].astype(jnp.float32)
            only(into(2, level), add_far)

            if level < 2:
                @pl.when(plane < last)
                def _():
                    sum_copy(piece, 3, level + 1).wait_recv()
                    own_sum[level, here] += down_buf[level, here].astype(jnp.float32)

            if level > 0:
                down_src[level - 1, here] = own_sum[level, here].astype(jnp.bfloat16)
                sum_copy(piece, 3, level).start()
            else:
                final[here] = own_sum[level, here].astype(jnp.bfloat16)
                for copy in final_copies(piece):
                    copy.start()

    def on_level(level, body):
        only(True if level == 0 else plane >= level, lambda: body(level))

    @pl.when(plane < 1)
    def _():
        slope_ref[:half, :] = jnp.zeros((half, slope_ref.shape[1]), slope_ref.dtype)

    @pl.when(plane < 2)
    def _():
        @pl.loop(0, PLANE - slot)
        def _(i):
            slope_ref[rows_of(PLANE + i, length), :] = jnp.zeros((length, slope_ref.shape[1]), slope_ref.dtype)

    on_level(2, compute)
    on_level(1, compute)
    on_level(2, to_far)
    near_rows()
    on_level(1, to_far)
    query_gradients()
    on_level(2, collect)
    on_level(0, compute)
    on_level(0, to_far)
    on_level(1, collect)
    on_level(0, collect)

    for level in range(3):
        @pl.when(plane >= level)
        def _():
            for kind in range(4):
                def wait_forward():
                    drain(whole_block, c_send.at[kind, level])
                if kind == 0:
                    if level < 2:
                        only(plane < last, wait_forward)
                elif kind == 3:
                    only(receives(1, level), wait_forward)
                else:
                    only(sends(kind, level), wait_forward)

            for kind in range(4):
                def wait_back():
                    drain(whole_block, r_send.at[kind, level])
                if kind == 3:
                    if level:
                        wait_back()
                elif kind == 2:
                    only(into(0, level), wait_back)
                else:
                    only(out_of(kind, level), wait_back)

    drain(pair_ref.at[:others, :], x_send)
    drain(weight_ref.at[: 2 * others, : group_size * width], q_send)
    for index, count in enumerate((tokens, others, others)):
        drain(query_ref.at[:count, :], dq_sems.at[index])
        drain(pair_ref.at[:count, :], f_sems.at[index])


def attention(queries, output_cotangent, keys, values, docs):
    heads = lax.axis_size("head")
    tokens, query_width = queries.shape
    length = tokens * heads
    width = keys.shape[1] // heads
    group_size = query_width // heads // width
    window = (SPAN + 1) * length
    anywhere = pl.BlockSpec(memory_space=pl.ANY)
    dma = pltpu.SemaphoreType.DMA
    rows = (length, query_width // heads)
    block = (length, 2 * width)
    bf16, f32 = jnp.bfloat16, jnp.float32
    narrow = jax.ShapeDtypeStruct((tokens, width * heads), bf16)
    return pl.pallas_call(
        functools.partial(attention_kernel, scaling=width ** (-0.5)),
        out_shape=(jax.ShapeDtypeStruct((tokens, query_width), bf16), narrow, narrow),
        in_specs=[anywhere] * 5,
        out_specs=(anywhere,) * 3,
        scratch_shapes=[
            pltpu.VMEM(rows, bf16),
            pltpu.VMEM(rows, bf16),
            pltpu.VMEM((SLOTS * length, 2 * width), bf16),
            pltpu.VMEM(docs.shape, docs.dtype),
            pltpu.VMEM((window, length), f32),
            pltpu.VMEM((width, window), bf16),
            pltpu.VMEM((window - PLANE * length, length), f32),
            pltpu.VMEM((window, group_size * length), f32),
            pltpu.VMEM((window, group_size * length), bf16),
            pltpu.VMEM((window, group_size * length), bf16),
            pltpu.VMEM((2, group_size * length, width), bf16),
            pltpu.VMEM((2, group_size * length, width), bf16),
            pltpu.VMEM(rows, bf16),
            pltpu.VMEM((group_size, 2, 3, 8, length), f32),
            pltpu.VMEM((8, group_size * length), f32),
            pltpu.VMEM((2, 8, group_size * length), f32),
            pltpu.VMEM((SLOTS * length, 2 * width), bf16),
            pltpu.VMEM((3, 2) + block, bf16),
            pltpu.VMEM((3,) + block, f32),
            pltpu.VMEM((3,) + block, bf16),
            pltpu.VMEM((3,) + block, bf16),
            pltpu.VMEM((2,) + block, bf16),
            pltpu.VMEM((2,) + block, bf16),
            pltpu.VMEM(block, bf16),
            dma((3,)), dma, dma((heads - 1,)), dma, dma((group_size,)),
            dma((4, 3)), dma((heads, 2, 3)), dma((2, 3)),
            dma((3,)), dma((4, 3)), dma((heads, 4, 3)), dma((3,)),
        ],
        compiler_params=pltpu.CompilerParams(
            collective_id=0, has_side_effects=True, vmem_limit_bytes=VMEM_LIMIT
        ),
    )(queries, output_cotangent, keys, values, docs)


def settle_kernel(dq_ref, dk_ref, dv_ref, dq_out, dk_out, dv_out, sems):
    copies = [
        pltpu.make_async_copy(source, target, sems.at[index])
        for index, (source, target) in enumerate(((dq_ref, dq_out), (dk_ref, dk_out), (dv_ref, dv_out)))
    ]
    for copy in copies:
        copy.start()
    for copy in copies:
        copy.wait()


def settle(*arrays):
    return pl.pallas_call(
        settle_kernel,
        out_shape=tuple(jax.ShapeDtypeStruct(array.shape, array.dtype) for array in arrays),
        in_specs=[pl.BlockSpec(memory_space=pltpu.VMEM)] * 3,
        out_specs=(pl.BlockSpec(memory_space=pl.ANY),) * 3,
        scratch_shapes=[pltpu.SemaphoreType.DMA((3,))],
    )(*arrays)


def on_device(queries, keys, values, output_cotangent, doc_ids):
    docs = doc_ids.reshape(-1, keys.shape[1] // lax.axis_size("head"))
    return settle(*attention(queries, output_cotangent, keys, values, docs))


def solution(mesh):
    rows = P(("ctx", "head"), None)
    return jax.shard_map(
        on_device,
        mesh=mesh,
        in_specs=(rows, rows, rows, rows, P()),
        out_specs=(rows, rows, rows),
        check_vma=False,
    )
```

```python
import functools
import math

import jax
import jax.numpy as jnp
from jax import lax
from jax.experimental import pallas as pl
from jax.experimental.pallas import tpu as pltpu
from jax.sharding import PartitionSpec as P

SPAN = 8
PLANE = SPAN // 2
SLOTS = SPAN + PLANE
EARLY = 5
RELAY = 2

masked_score = -1e30
LOG2E = math.log2(math.e)
VMEM_LIMIT = 56 * 1024 * 1024
MESH = pl.DeviceIdType.MESH


def greet(partners):
    barrier = pltpu.get_barrier_semaphore()
    for partner in partners:
        pl.semaphore_signal(barrier, inc=1, device_id=partner, device_id_type=MESH)
    pl.semaphore_wait(barrier, len(partners))


def places():
    ctx, head = lax.axis_index("ctx"), lax.axis_index("head")
    count = lax.axis_size("ctx")
    slot = lax.rem(ctx, PLANE)
    base = ctx - slot
    up = lax.rem(ctx + PLANE, count)
    down = lax.rem(ctx + count - PLANE, count)
    far = lax.rem(slot + PLANE // 2, PLANE)
    near = slot + 1 - 2 * lax.rem(slot, 2)
    diagonal = lax.rem(near + PLANE // 2, PLANE)
    return ctx, head, slot, base, up, down, near, far, diagonal


def head_peers(head):
    count = lax.axis_size("head")
    return [lax.rem(head + step, count) for step in range(1, count)]


def rows_of(index, length):
    return pl.ds(pl.multiple_of(index * length, length), length)


def pieces_of(tokens):
    return max(1, min(4, tokens // 16))


def fold(x, op):
    return op(x.reshape(-1, 8, x.shape[-1]), axis=0)


def drain(ref, sem):
    pltpu.make_async_copy(ref, ref, sem).wait()


def attention_kernel(
    query_in, grad_in, key_in, value_in, doc_in, dq_out, dk_out, dv_out,
    query_ref, grad_ref, pair_ref, doc_ref, bias_ref, key_t_ref,
    score_ref, product_ref, weight_ref, slope_ref, query_rows, grad_rows, dq_ref, stat_ref, dot_ref, factor_ref,
    part_ref, near_buf, own_sum, far_sum, far_buf, down_src, down_buf, final,
    local_sems, x_send, x_recv, q_send, q_recv, c_send, c_recv, c_block,
    dq_sems, r_send, r_recv, f_sems, *, scaling
):
    ctx, head, slot, base, up, down, near, far, diagonal = places()
    peers = head_peers(head)
    tokens = key_in.shape[0]
    length = tokens * lax.axis_size("head")
    plane = ctx // PLANE
    last = lax.axis_size("ctx") // PLANE - 1
    low, not_low = slot < PLANE // 2, slot >= PLANE // 2
    even, not_even = lax.rem(slot, 2) == 0, lax.rem(slot, 2) == 1
    width = pair_ref.shape[1] // 2
    others = len(peers) * tokens
    doc_copy = pltpu.make_async_copy(doc_in, doc_ref, local_sems.at[2])
    doc_copy.start()
    greet(
        [{"head": peer} for peer in peers]
        + [{"ctx": up}, {"ctx": down}, {"ctx": base + near}, {"ctx": base + far}]
    )
    rows_here = pl.ds(pl.multiple_of(head * tokens, tokens), tokens)
    own_rows = pl.ds(pl.multiple_of((slot + SPAN) * length + head * tokens, tokens), tokens)
    lanes_of = (slice(0, width), slice(width, 2 * width))
    for array, source in enumerate((key_in, value_in)):
        pltpu.make_async_copy(
            source.at[:, rows_of(head, width)], pair_ref.at[own_rows, lanes_of[array]], local_sems.at[0]
        ).start()
        for step, peer in enumerate(peers):
            pltpu.make_async_remote_copy(
                src_ref=source.at[:, rows_of(peer, width)],
                dst_ref=pair_ref.at[own_rows, lanes_of[array]],
                send_sem=x_send,
                recv_sem=x_recv.at[step],
                device_id={"head": peer},
                device_id_type=MESH,
            ).start()
    for source, target in ((query_in, query_ref), (grad_in, grad_ref)):
        pltpu.make_async_copy(
            source.at[:, rows_of(head, target.shape[1])], target.at[rows_here, :], local_sems.at[1]
        ).start()
    group_size = query_ref.shape[1] // width

    def head_copies(g):
        copies = []
        for source, target in ((query_in, query_ref), (grad_in, grad_ref)):
            for step, peer in enumerate(peers):
                columns = pl.ds(pl.multiple_of((peer * group_size + g) * width, width), width)
                copies.append(
                    pltpu.make_async_remote_copy(
                        src_ref=source.at[:, columns],
                        dst_ref=target.at[rows_here, pl.ds(pl.multiple_of(g * width, width), width)],
                        send_sem=q_send,
                        recv_sem=q_recv.at[g],
                        device_id={"head": peer},
                        device_id_type=MESH,
                    )
                )
        return copies

    @pl.loop(0, group_size)
    def _(g):
        for copy in head_copies(g):
            copy.start()

    order = [head] + [lax.rem(head + len(peers) + 1 - step, len(peers) + 1) for step in range(1, len(peers) + 1)]
    cut = pieces_of(tokens)
    rows_each = tokens // cut
    pieces = range(len(order) * cut)

    def piece_start(parts_order, piece):
        return parts_order[piece // cut] * tokens + piece % cut * rows_each

    def sends(kind, level):
        if level == 1:
            return True
        return ((not_low, low), (not_even, even), (low, not_low))[kind - 1][0 if level == 2 else 1]

    def receives(kind, level):
        if level == 1:
            return True
        return ((low, not_low), (even, not_even), (low, not_low))[kind - 1][0 if level == 2 else 1]

    def only(condition, body):
        if condition is True:
            body()
        else:
            pl.when(condition)(body)

    def copy_of(piece, kind, level):
        block, shift, partner = (
            (slot, 1, up), (slot, 0, base + far), (slot, 0, base + near), (far, 0, base + near)
        )[kind]
        offset = block * length + piece_start(order, piece)
        source = pl.ds(pl.multiple_of((2 - level) * PLANE * length + offset, rows_each), rows_each)
        landing = pl.ds(pl.multiple_of((2 - level - shift) * PLANE * length + offset, rows_each), rows_each)
        return pltpu.make_async_remote_copy(
            src_ref=pair_ref.at[source, :],
            dst_ref=pair_ref.at[landing, :],
            send_sem=c_send.at[kind, level],
            recv_sem=c_recv.at[piece, kind, level] if kind < 2 else c_block.at[kind - 2, level],
            device_id={"ctx": partner},
            device_id_type=MESH,
        )

    def spread(piece, level):
        if level < 2:
            only(plane < last, lambda: copy_of(piece, 0, level).start())
        only(sends(1, level), lambda: copy_of(piece, 1, level).start())
        only(sends(2, level), lambda: copy_of(piece, 2, level).start())

    def relay(piece, level):
        def body():
            copy_of(piece, 1, level).wait_recv()
            copy_of(piece, 3, level).start()
        only(receives(1, level), body)

    whole_block = pair_ref.at[:length, :]
    for piece in pieces:
        if piece == 0:
            drain(pair_ref.at[:tokens, :], local_sems.at[0])
        elif piece % cut == 0:
            drain(pair_ref.at[:tokens, :], x_recv.at[piece // cut - 1])
        spread(piece, 0)
    doc_copy.wait()
    window = bias_ref.shape[0]
    own_block = ctx
    mixed = SPAN + 1 - PLANE
    places_of = [PLANE + i for i in range(PLANE)] + [
        slot + i + jnp.where(i >= PLANE - slot, PLANE, 0) for i in range(mixed)
    ]
    lanes = doc_ref.shape[1]
    half = PLANE * length
    own_row = own_block * (length // lanes)
    query_docs = jnp.concatenate(
        [doc_ref[pl.ds(own_row + i, 1), :] for i in range(length // lanes)], axis=1
    )
    query_pos = own_block * length + lax.broadcasted_iota(jnp.int32, (lanes, length), 1)
    for block, spot in enumerate(places_of):
        for i in range(length // lanes):
            key_block = base - SPAN + spot
            row = jnp.maximum(key_block * (length // lanes) + i, 0)
            key_docs = jnp.broadcast_to(doc_ref[pl.ds(row, 1), :], (lanes, lanes)).T
            key_docs = jnp.concatenate([key_docs] * (length // lanes), axis=1)
            key_pos = key_block * length + i * lanes + lax.broadcasted_iota(jnp.int32, (lanes, length), 0)
            allowed = (key_docs == query_docs) & (key_pos <= query_pos) & (key_pos >= 0)
            first = block * length + i * lanes
            bias_ref[first : first + lanes, :] = jnp.where(allowed, 0.0, masked_score)
    for level in (1, 2):
        @pl.when(plane < level)
        def _():
            absent = pl.ds((2 - level) * PLANE * length, PLANE * length)
            pair_ref[absent, :] = jnp.zeros((PLANE * length, 2 * width), pair_ref.dtype)
    for level in (1, 2):
        for piece in pieces:
            @pl.when(plane >= level)
            def _():
                copy_of(piece, 0, level - 1).wait_recv()
                spread(piece, level)

            only(True if level == 1 else plane >= 1, lambda: relay(piece, level - 1))

    def arrived(level):
        @pl.when(plane >= level)
        def _():
            for kind in (2, 3):
                only(receives(kind, level), lambda: drain(whole_block, c_block.at[kind - 2, level]))

    contract_last = (((1,), (1,)), ((), ()))

    def columns_of(g, size):
        return pl.ds(pl.multiple_of(g * size, size), size)

    def softmax(g, group):
        blocks = range(PLANE) if group == 0 else range(PLANE, SPAN + 1)
        first = blocks[0] * length
        query = query_ref[:, columns_of(g, width)]
        grad = grad_ref[:, columns_of(g, width)]
        places_g = columns_of(g, length)
        top = None
        for j in blocks:
            here = slice(j * length, (j + 1) * length)
            slots = slice(j * length - first, (j + 1) * length - first)
            there = rows_of(places_of[j], length)
            scores = lax.dot_general(pair_ref[there, :width], query, contract_last, preferred_element_type=jnp.float32)
            scores = scores * (scaling * LOG2E) + bias_ref[here, :]
            score_ref[slots, :] = scores
            block_top = fold(scores, jnp.max)
            top = block_top if top is None else jnp.maximum(top, block_top)
        top = jnp.max(top, axis=0, keepdims=True)
        total = jnp.zeros((8, length), jnp.float32)
        dots = jnp.zeros((8, length), jnp.float32)
        for j in blocks:
            here = slice(j * length, (j + 1) * length)
            slots = slice(j * length - first, (j + 1) * length - first)
            there = rows_of(places_of[j], length)
            powers = jnp.exp2(score_ref[slots, :] - top)
            weight_ref[here, places_g] = powers.astype(jnp.bfloat16)
            total = total + fold(powers, jnp.sum)
            product = lax.dot_general(pair_ref[there, width:], grad, contract_last, preferred_element_type=jnp.float32)
            product_ref[here, places_g] = product
            dots = dots + fold(powers * product, jnp.sum)
        for index, value in enumerate((top, jnp.sum(total, axis=0, keepdims=True), jnp.sum(dots, axis=0, keepdims=True))):
            stat_ref[g, group, index] = jnp.broadcast_to(value, (8, length))

    def join(g):
        places_g = columns_of(g, length)
        query = query_ref[:, columns_of(g, width)].astype(jnp.float32)
        grad = grad_ref[:, columns_of(g, width)].astype(jnp.float32)
        tops = [stat_ref[g, group, 0] for group in range(2)]
        top = jnp.maximum(*tops)
        powers = [jnp.exp2(value - top) for value in tops]
        inverse = 1.0 / sum(power * stat_ref[g, group, 1] for group, power in enumerate(powers))
        dot_ref[:, places_g] = sum(power * stat_ref[g, group, 2] for group, power in enumerate(powers)) * inverse
        for group, power in enumerate(powers):
            factor = power * inverse
            factor_ref[group, :, places_g] = factor * scaling
            by_row = jnp.broadcast_to(factor[:1], (width, length)).T
            grad_rows[group, places_g, :] = (grad * by_row).astype(jnp.bfloat16)
            query_rows[group, places_g, :] = (query * by_row).astype(jnp.bfloat16)

    def head_here(g):
        drain(query_rows.at[0, : 2 * others, :], q_recv.at[g])

    drain(query_ref.at[: 2 * tokens, :], local_sems.at[1])
    arrived(0)
    arrived(1)
    early = min(EARLY, group_size)

    @pl.loop(0, early)
    def _(g):
        head_here(g)
        softmax(g, 0)

        @pl.when((g == RELAY) & (plane >= 2))
        def _():
            for piece in pieces:
                relay(piece, 2)

    arrived(2)

    @pl.loop(0, early)
    def _(g):
        softmax(g, 1)
        join(g)

    @pl.loop(early, group_size)
    def _(g):
        head_here(g)
        softmax(g, 0)
        softmax(g, 1)
        join(g)

    def dq_copies(g):
        columns = columns_of(g, width)
        landing = pl.ds(pl.multiple_of((head * group_size + g) * width, width), width)
        local = pltpu.make_async_copy(dq_ref.at[rows_here, columns], dq_out.at[:, landing], dq_sems.at[0])
        return [local] + [
            pltpu.make_async_remote_copy(
                src_ref=dq_ref.at[rows_of(peer, tokens), columns],
                dst_ref=dq_out.at[:, landing],
                send_sem=dq_sems.at[1],
                recv_sem=dq_sems.at[2],
                device_id={"head": peer},
                device_id_type=MESH,
            )
            for peer in peers
        ]

    def query_gradients():
        for j, spot in enumerate(places_of):
            key_t_ref[:, j * length : (j + 1) * length] = pair_ref[rows_of(spot, length), :width].T

        @pl.loop(0, group_size)
        def _(g):
            places_g = columns_of(g, length)
            dq_t = jnp.zeros((width, length), jnp.float32)
            for group, here in enumerate((slice(0, half), slice(half, window))):
                part = jnp.dot(key_t_ref[:, here], slope_ref[here, places_g], preferred_element_type=jnp.float32)
                dq_t = dq_t + part * factor_ref[group, :1, places_g]
            dq_ref[:, columns_of(g, width)] = dq_t.T.astype(jnp.bfloat16)
            for copy in dq_copies(g):
                copy.start()

    back = peers + [head]

    def level_rows(level, position, piece):
        start = ((2 - level) * PLANE + position) * length + piece_start(back, piece)
        return pl.ds(pl.multiple_of(start, rows_each), rows_each)

    def slab(piece):
        return pl.ds(pl.multiple_of(piece_start(back, piece), rows_each), rows_each)

    def sum_copy(piece, kind, level):
        here = slab(piece)
        source, target, place = (
            (lambda: part_ref.at[level_rows(level, diagonal, piece), :], lambda: near_buf.at[level, 0, here], {"ctx": base + near}),
            (lambda: part_ref.at[level_rows(level, near, piece), :], lambda: near_buf.at[level, 1, here], {"ctx": base + near}),
            (lambda: far_sum.at[level, here], lambda: far_buf.at[level, here], {"ctx": base + far}),
            (lambda: down_src.at[level - 1, here], lambda: down_buf.at[level - 1, here], {"ctx": down}),
        )[kind]
        return pltpu.make_async_remote_copy(
            src_ref=source(),
            dst_ref=target(),
            send_sem=r_send.at[kind, level],
            recv_sem=r_recv.at[piece, kind, level],
            device_id=place,
            device_id_type=MESH,
        )

    def out_of(kind, level):
        if level == 1:
            return True
        return ((low, not_low), (even, not_even), (low, not_low))[kind][0 if level == 2 else 1]

    def into(kind, level):
        if level == 1:
            return True
        return ((low, not_low), (not_even, even), (not_low, low))[kind][0 if level == 2 else 1]

    def final_copies(piece):
        copies = []
        for array, target in enumerate((dk_out, dv_out)):
            source = final.at[slab(piece), lanes_of[array]]
            cols = rows_of(head, width)
            owner = piece // cut
            target = target.at[piece % cut * rows_each : (piece % cut + 1) * rows_each, :]
            if owner == len(peers):
                copies.append(pltpu.make_async_copy(source, target.at[:, cols], f_sems.at[0]))
            else:
                copies.append(
                    pltpu.make_async_remote_copy(
                        src_ref=source,
                        dst_ref=target.at[:, cols],
                        send_sem=f_sems.at[1],
                        recv_sem=f_sems.at[2],
                        device_id={"head": peers[owner]},
                        device_id_type=MESH,
                    )
                )
        return copies

    def slopes(here):
        for g in range(group_size):
            places_g = slice(g * length, (g + 1) * length)
            slope_ref[here, places_g] = (
                weight_ref[here, places_g].astype(jnp.float32)
                * (product_ref[here, places_g] - dot_ref[:1, places_g])
            ).astype(jnp.bfloat16)

    def sums(here, there, group):
        part_ref[there, :width] = (
            jnp.dot(slope_ref[here, :], query_rows[group], preferred_element_type=jnp.float32) * scaling
        ).astype(jnp.bfloat16)
        part_ref[there, width:] = jnp.dot(
            weight_ref[here, :], grad_rows[group], preferred_element_type=jnp.float32
        ).astype(jnp.bfloat16)

    def near_rows():
        @pl.loop(0, slot + 1)
        def _(i):
            slopes(rows_of(SPAN - slot + i, length))

    def start_sums(kind, level):
        def body():
            for piece in pieces:
                sum_copy(piece, kind, level).start()
        only(out_of(kind, level), body)

    def send_far(level):
        for piece in pieces:
            here = slab(piece)
            sum_copy(piece, 0, level).wait_recv()
            far_sum[level, here] = (
                part_ref[level_rows(level, far, piece), :].astype(jnp.float32)
                + near_buf[level, 0, here].astype(jnp.float32)
            ).astype(jnp.bfloat16)
            sum_copy(piece, 2, level).start()

    def to_far(level):
        only(into(0, level), lambda: send_far(level))

    def compute(level):
        if level == 1:
            for i in range(PLANE):
                here = slice(i * length, (i + 1) * length)
                slopes(here)
                sums(here, slice((PLANE + i) * length, (PLANE + i + 1) * length), 0)
            for kind in (0, 1):
                start_sums(kind, 1)
        elif level == 2:
            @pl.loop(0, PLANE - slot)
            def _(i):
                spot = slot + i
                turned = jnp.where(i == 0, diagonal, jnp.where(i == 1, far, slot + i - PLANE // 2))
                spot = jnp.where(low, turned, spot)
                here = rows_of(PLANE - slot + spot, length)
                slopes(here)
                sums(here, rows_of(spot, length), 1)

                @pl.when(low & (i == 0))
                def _():
                    for piece in pieces:
                        sum_copy(piece, 0, 2).start()

                @pl.when(low & (i == 1))
                def _():
                    send_far(2)

            start_sums(1, 2)
        else:
            @pl.loop(0, slot + 1)
            def _(i):
                sums(rows_of(SPAN - slot + i, length), rows_of(2 * PLANE + i, length), 1)

            for kind in (0, 1):
                start_sums(kind, 0)

    def collect(level):
        for piece in pieces:
            here = slab(piece)
            own_sum[level, here] = part_ref[level_rows(level, slot, piece), :].astype(jnp.float32)

            def add_near():
                sum_copy(piece, 1, level).wait_recv()
                own_sum[level, here] += near_buf[level, 1, here].astype(jnp.float32)
            only(into(1, level), add_near)

            def add_far():
                sum_copy(piece, 2, level).wait_recv()
                own_sum[level, here] += far_buf[level, here].astype(jnp.float32)
            only(into(2, level), add_far)

            if level < 2:
                @pl.when(plane < last)
                def _():
                    sum_copy(piece, 3, level + 1).wait_recv()
                    own_sum[level, here] += down_buf[level, here].astype(jnp.float32)

            if level > 0:
                down_src[level - 1, here] = own_sum[level, here].astype(jnp.bfloat16)
                sum_copy(piece, 3, level).start()
            else:
                final[here] = own_sum[level, here].astype(jnp.bfloat16)
                for copy in final_copies(piece):
                    copy.start()

    def on_level(level, body):
        only(True if level == 0 else plane >= level, lambda: body(level))

    @pl.when(plane < 1)
    def _():
        slope_ref[:half, :] = jnp.zeros((half, slope_ref.shape[1]), slope_ref.dtype)

    @pl.when(plane < 2)
    def _():
        @pl.loop(0, PLANE - slot)
        def _(i):
            slope_ref[rows_of(PLANE + i, length), :] = jnp.zeros((length, slope_ref.shape[1]), slope_ref.dtype)

    on_level(2, compute)
    on_level(1, compute)
    near_rows()
    on_level(1, to_far)
    on_level(0, compute)
    on_level(2, collect)
    on_level(0, to_far)
    query_gradients()
    on_level(1, collect)
    on_level(0, collect)

    for level in range(3):
        @pl.when(plane >= level)
        def _():
            for kind in range(4):
                def wait_forward():
                    drain(whole_block, c_send.at[kind, level])
                if kind == 0:
                    if level < 2:
                        only(plane < last, wait_forward)
                elif kind == 3:
                    only(receives(1, level), wait_forward)
                else:
                    only(sends(kind, level), wait_forward)

            for kind in range(4):
                def wait_back():
                    drain(whole_block, r_send.at[kind, level])
                if kind == 3:
                    if level:
                        wait_back()
                elif kind == 2:
                    only(into(0, level), wait_back)
                else:
                    only(out_of(kind, level), wait_back)

    drain(pair_ref.at[:others, :], x_send)
    drain(weight_ref.at[: 2 * others, : group_size * width], q_send)
    for index, count in enumerate((tokens, others, others)):
        drain(query_ref.at[:count, :], dq_sems.at[index])
        drain(pair_ref.at[:count, :], f_sems.at[index])


def attention(queries, output_cotangent, keys, values, docs):
    heads = lax.axis_size("head")
    tokens, query_width = queries.shape
    length = tokens * heads
    width = keys.shape[1] // heads
    group_size = query_width // heads // width
    window = (SPAN + 1) * length
    anywhere = pl.BlockSpec(memory_space=pl.ANY)
    dma = pltpu.SemaphoreType.DMA
    rows = (length, query_width // heads)
    block = (length, 2 * width)
    bf16, f32 = jnp.bfloat16, jnp.float32
    narrow = jax.ShapeDtypeStruct((tokens, width * heads), bf16)
    return pl.pallas_call(
        functools.partial(attention_kernel, scaling=width ** (-0.5)),
        out_shape=(jax.ShapeDtypeStruct((tokens, query_width), bf16), narrow, narrow),
        in_specs=[anywhere] * 5,
        out_specs=(anywhere,) * 3,
        scratch_shapes=[
            pltpu.VMEM(rows, bf16),
            pltpu.VMEM(rows, bf16),
            pltpu.VMEM((SLOTS * length, 2 * width), bf16),
            pltpu.VMEM(docs.shape, docs.dtype),
            pltpu.VMEM((window, length), f32),
            pltpu.VMEM((width, window), bf16),
            pltpu.VMEM((window - PLANE * length, length), f32),
            pltpu.VMEM((window, group_size * length), f32),
            pltpu.VMEM((window, group_size * length), bf16),
            pltpu.VMEM((window, group_size * length), bf16),
            pltpu.VMEM((2, group_size * length, width), bf16),
            pltpu.VMEM((2, group_size * length, width), bf16),
            pltpu.VMEM(rows, bf16),
            pltpu.VMEM((group_size, 2, 3, 8, length), f32),
            pltpu.VMEM((8, group_size * length), f32),
            pltpu.VMEM((2, 8, group_size * length), f32),
            pltpu.VMEM((SLOTS * length, 2 * width), bf16),
            pltpu.VMEM((3, 2) + block, bf16),
            pltpu.VMEM((3,) + block, f32),
            pltpu.VMEM((3,) + block, bf16),
            pltpu.VMEM((3,) + block, bf16),
            pltpu.VMEM((2,) + block, bf16),
            pltpu.VMEM((2,) + block, bf16),
            pltpu.VMEM(block, bf16),
            dma((3,)), dma, dma((heads - 1,)), dma, dma((group_size,)),
            dma((4, 3)), dma((heads * pieces_of(tokens), 2, 3)), dma((2, 3)),
            dma((3,)), dma((4, 3)), dma((heads * pieces_of(tokens), 4, 3)), dma((3,)),
        ],
        compiler_params=pltpu.CompilerParams(
            collective_id=0, has_side_effects=True, vmem_limit_bytes=VMEM_LIMIT
        ),
    )(queries, output_cotangent, keys, values, docs)


def settle_kernel(dq_ref, dk_ref, dv_ref, dq_out, dk_out, dv_out, sems):
    copies = [
        pltpu.make_async_copy(source, target, sems.at[index])
        for index, (source, target) in enumerate(((dq_ref, dq_out), (dk_ref, dk_out), (dv_ref, dv_out)))
    ]
    for copy in copies:
        copy.start()
    for copy in copies:
        copy.wait()


def settle(*arrays):
    return pl.pallas_call(
        settle_kernel,
        out_shape=tuple(jax.ShapeDtypeStruct(array.shape, array.dtype) for array in arrays),
        in_specs=[pl.BlockSpec(memory_space=pltpu.VMEM)] * 3,
        out_specs=(pl.BlockSpec(memory_space=pl.ANY),) * 3,
        scratch_shapes=[pltpu.SemaphoreType.DMA((3,))],
    )(*arrays)


def on_device(queries, keys, values, output_cotangent, doc_ids):
    docs = doc_ids.reshape(-1, keys.shape[1] // lax.axis_size("head"))
    return settle(*attention(queries, output_cotangent, keys, values, docs))


def solution(mesh):
    rows = P(("ctx", "head"), None)
    return jax.shard_map(
        on_device,
        mesh=mesh,
        in_specs=(rows, rows, rows, rows, P()),
        out_specs=(rows, rows, rows),
        check_vma=False,
    )
```

```python
import functools
import math

import jax
import jax.numpy as jnp
from jax import lax
from jax.experimental import pallas as pl
from jax.experimental.pallas import tpu as pltpu
from jax.sharding import PartitionSpec as P

SPAN = 8
PLANE = SPAN // 2
SLOTS = SPAN + PLANE
EARLY = 5
RELAY = 2

masked_score = -1e30
LOG2E = math.log2(math.e)
VMEM_LIMIT = 56 * 1024 * 1024
MESH = pl.DeviceIdType.MESH


def greet(partners):
    barrier = pltpu.get_barrier_semaphore()
    for partner in partners:
        pl.semaphore_signal(barrier, inc=1, device_id=partner, device_id_type=MESH)
    pl.semaphore_wait(barrier, len(partners))


def places():
    ctx, head = lax.axis_index("ctx"), lax.axis_index("head")
    count = lax.axis_size("ctx")
    slot = lax.rem(ctx, PLANE)
    base = ctx - slot
    up = lax.rem(ctx + PLANE, count)
    down = lax.rem(ctx + count - PLANE, count)
    far = lax.rem(slot + PLANE // 2, PLANE)
    near = slot + 1 - 2 * lax.rem(slot, 2)
    diagonal = lax.rem(near + PLANE // 2, PLANE)
    return ctx, head, slot, base, up, down, near, far, diagonal


def head_peers(head):
    count = lax.axis_size("head")
    return [lax.rem(head + step, count) for step in range(1, count)]


def rows_of(index, length):
    return pl.ds(pl.multiple_of(index * length, length), length)


def pieces_of(tokens):
    return max(1, min(4, tokens // 16))


def fold(x, op):
    return op(x.reshape(-1, 8, x.shape[-1]), axis=0)


def drain(ref, sem):
    pltpu.make_async_copy(ref, ref, sem).wait()


def attention_kernel(
    query_in, grad_in, key_in, value_in, doc_in, dq_out, dk_out, dv_out,
    query_ref, grad_ref, pair_ref, doc_ref, bias_ref, key_t_ref,
    score_ref, product_ref, weight_ref, slope_ref, query_rows, grad_rows, dq_ref, stat_ref, dot_ref, factor_ref,
    part_ref, near_buf, own_sum, far_sum, far_buf, down_src, down_buf, final,
    local_sems, x_send, x_recv, q_send, q_recv, c_send, c_recv, c_block,
    dq_sems, r_send, r_recv, f_sems, *, scaling
):
    ctx, head, slot, base, up, down, near, far, diagonal = places()
    peers = head_peers(head)
    tokens = key_in.shape[0]
    length = tokens * lax.axis_size("head")
    plane = ctx // PLANE
    last = lax.axis_size("ctx") // PLANE - 1
    low, not_low = slot < PLANE // 2, slot >= PLANE // 2
    even, not_even = lax.rem(slot, 2) == 0, lax.rem(slot, 2) == 1
    width = pair_ref.shape[1] // 2
    others = len(peers) * tokens
    doc_copy = pltpu.make_async_copy(doc_in, doc_ref, local_sems.at[2])
    doc_copy.start()
    greet(
        [{"head": peer} for peer in peers]
        + [{"ctx": up}, {"ctx": down}, {"ctx": base + near}, {"ctx": base + far}]
    )
    rows_here = pl.ds(pl.multiple_of(head * tokens, tokens), tokens)
    own_rows = pl.ds(pl.multiple_of((slot + SPAN) * length + head * tokens, tokens), tokens)
    lanes_of = (slice(0, width), slice(width, 2 * width))
    for array, source in enumerate((key_in, value_in)):
        pltpu.make_async_copy(
            source.at[:, rows_of(head, width)], pair_ref.at[own_rows, lanes_of[array]], local_sems.at[0]
        ).start()
        for step, peer in enumerate(peers):
            pltpu.make_async_remote_copy(
                src_ref=source.at[:, rows_of(peer, width)],
                dst_ref=pair_ref.at[own_rows, lanes_of[array]],
                send_sem=x_send,
                recv_sem=x_recv.at[step],
                device_id={"head": peer},
                device_id_type=MESH,
            ).start()
    for source, target in ((query_in, query_ref), (grad_in, grad_ref)):
        pltpu.make_async_copy(
            source.at[:, rows_of(head, target.shape[1])], target.at[rows_here, :], local_sems.at[1]
        ).start()
    group_size = query_ref.shape[1] // width

    def head_copies(g):
        copies = []
        for source, target in ((query_in, query_ref), (grad_in, grad_ref)):
            for step, peer in enumerate(peers):
                columns = pl.ds(pl.multiple_of((peer * group_size + g) * width, width), width)
                copies.append(
                    pltpu.make_async_remote_copy(
                        src_ref=source.at[:, columns],
                        dst_ref=target.at[rows_here, pl.ds(pl.multiple_of(g * width, width), width)],
                        send_sem=q_send,
                        recv_sem=q_recv.at[g],
                        device_id={"head": peer},
                        device_id_type=MESH,
                    )
                )
        return copies

    @pl.loop(0, group_size)
    def _(g):
        for copy in head_copies(g):
            copy.start()

    order = [head] + [lax.rem(head + len(peers) + 1 - step, len(peers) + 1) for step in range(1, len(peers) + 1)]
    cut = pieces_of(tokens)
    rows_each = tokens // cut
    pieces = range(len(order) * cut)

    def piece_start(parts_order, piece):
        return parts_order[piece // cut] * tokens + piece % cut * rows_each

    def sends(kind, level):
        if level == 1:
            return True
        return ((not_low, low), (not_even, even), (low, not_low))[kind - 1][0 if level == 2 else 1]

    def receives(kind, level):
        if level == 1:
            return True
        return ((low, not_low), (even, not_even), (low, not_low))[kind - 1][0 if level == 2 else 1]

    def only(condition, body):
        if condition is True:
            body()
        else:
            pl.when(condition)(body)

    def copy_of(piece, kind, level):
        block, shift, partner = (
            (slot, 1, up), (slot, 0, base + far), (slot, 0, base + near), (far, 0, base + near)
        )[kind]
        offset = block * length + piece_start(order, piece)
        source = pl.ds(pl.multiple_of((2 - level) * PLANE * length + offset, rows_each), rows_each)
        landing = pl.ds(pl.multiple_of((2 - level - shift) * PLANE * length + offset, rows_each), rows_each)
        return pltpu.make_async_remote_copy(
            src_ref=pair_ref.at[source, :],
            dst_ref=pair_ref.at[landing, :],
            send_sem=c_send.at[kind, level],
            recv_sem=c_recv.at[piece, kind, level] if kind < 2 else c_block.at[kind - 2, level],
            device_id={"ctx": partner},
            device_id_type=MESH,
        )

    def spread(piece, level):
        if level < 2:
            only(plane < last, lambda: copy_of(piece, 0, level).start())
        only(sends(1, level), lambda: copy_of(piece, 1, level).start())
        only(sends(2, level), lambda: copy_of(piece, 2, level).start())

    def relay(piece, level):
        def body():
            copy_of(piece, 1, level).wait_recv()
            copy_of(piece, 3, level).start()
        only(receives(1, level), body)

    whole_block = pair_ref.at[:length, :]
    for piece in pieces:
        if piece == 0:
            drain(pair_ref.at[:tokens, :], local_sems.at[0])
        elif piece % cut == 0:
            drain(pair_ref.at[:tokens, :], x_recv.at[piece // cut - 1])
        spread(piece, 0)
    doc_copy.wait()
    window = bias_ref.shape[0]
    own_block = ctx
    mixed = SPAN + 1 - PLANE
    places_of = [PLANE + i for i in range(PLANE)] + [
        slot + i + jnp.where(i >= PLANE - slot, PLANE, 0) for i in range(mixed)
    ]
    lanes = doc_ref.shape[1]
    half = PLANE * length
    own_row = own_block * (length // lanes)
    query_docs = jnp.concatenate(
        [doc_ref[pl.ds(own_row + i, 1), :] for i in range(length // lanes)], axis=1
    )
    query_pos = own_block * length + lax.broadcasted_iota(jnp.int32, (lanes, length), 1)
    for block, spot in enumerate(places_of):
        for i in range(length // lanes):
            key_block = base - SPAN + spot
            row = jnp.maximum(key_block * (length // lanes) + i, 0)
            key_docs = jnp.broadcast_to(doc_ref[pl.ds(row, 1), :], (lanes, lanes)).T
            key_docs = jnp.concatenate([key_docs] * (length // lanes), axis=1)
            key_pos = key_block * length + i * lanes + lax.broadcasted_iota(jnp.int32, (lanes, length), 0)
            allowed = (key_docs == query_docs) & (key_pos <= query_pos) & (key_pos >= 0)
            first = block * length + i * lanes
            bias_ref[first : first + lanes, :] = jnp.where(allowed, 0.0, masked_score)
    for level in (1, 2):
        @pl.when(plane < level)
        def _():
            absent = pl.ds((2 - level) * PLANE * length, PLANE * length)
            pair_ref[absent, :] = jnp.zeros((PLANE * length, 2 * width), pair_ref.dtype)
    for level in (1, 2):
        for piece in pieces:
            @pl.when(plane >= level)
            def _():
                copy_of(piece, 0, level - 1).wait_recv()
                spread(piece, level)

            only(True if level == 1 else plane >= 1, lambda: relay(piece, level - 1))

    def arrived(level):
        @pl.when(plane >= level)
        def _():
            for kind in (2, 3):
                only(receives(kind, level), lambda: drain(whole_block, c_block.at[kind - 2, level]))

    contract_last = (((1,), (1,)), ((), ()))

    def columns_of(g, size):
        return pl.ds(pl.multiple_of(g * size, size), size)

    def softmax(g, group):
        blocks = range(PLANE) if group == 0 else range(PLANE, SPAN + 1)
        first = blocks[0] * length
        query = query_ref[:, columns_of(g, width)]
        grad = grad_ref[:, columns_of(g, width)]
        places_g = columns_of(g, length)
        top = None
        for j in blocks:
            here = slice(j * length, (j + 1) * length)
            slots = slice(j * length - first, (j + 1) * length - first)
            there = rows_of(places_of[j], length)
            scores = lax.dot_general(pair_ref[there, :width], query, contract_last, preferred_element_type=jnp.float32)
            scores = scores * (scaling * LOG2E) + bias_ref[here, :]
            score_ref[slots, :] = scores
            block_top = fold(scores, jnp.max)
            top = block_top if top is None else jnp.maximum(top, block_top)
        top = jnp.max(top, axis=0, keepdims=True)
        total = jnp.zeros((8, length), jnp.float32)
        dots = jnp.zeros((8, length), jnp.float32)
        for j in blocks:
            here = slice(j * length, (j + 1) * length)
            slots = slice(j * length - first, (j + 1) * length - first)
            there = rows_of(places_of[j], length)
            powers = jnp.exp2(score_ref[slots, :] - top)
            weight_ref[here, places_g] = powers.astype(jnp.bfloat16)
            total = total + fold(powers, jnp.sum)
            product = lax.dot_general(pair_ref[there, width:], grad, contract_last, preferred_element_type=jnp.float32)
            product_ref[here, places_g] = product
            dots = dots + fold(powers * product, jnp.sum)
        for index, value in enumerate((top, jnp.sum(total, axis=0, keepdims=True), jnp.sum(dots, axis=0, keepdims=True))):
            stat_ref[g, group, index] = jnp.broadcast_to(value, (8, length))

    def join(g):
        places_g = columns_of(g, length)
        query = query_ref[:, columns_of(g, width)].astype(jnp.float32)
        grad = grad_ref[:, columns_of(g, width)].astype(jnp.float32)
        tops = [stat_ref[g, group, 0] for group in range(2)]
        top = jnp.maximum(*tops)
        powers = [jnp.exp2(value - top) for value in tops]
        inverse = 1.0 / sum(power * stat_ref[g, group, 1] for group, power in enumerate(powers))
        dot_ref[:, places_g] = sum(power * stat_ref[g, group, 2] for group, power in enumerate(powers)) * inverse
        for group, power in enumerate(powers):
            factor = power * inverse
            factor_ref[group, :, places_g] = factor * scaling
            by_row = jnp.broadcast_to(factor[:1], (width, length)).T
            grad_rows[group, places_g, :] = (grad * by_row).astype(jnp.bfloat16)
            query_rows[group, places_g, :] = (query * by_row).astype(jnp.bfloat16)

    def head_here(g):
        drain(query_rows.at[0, : 2 * others, :], q_recv.at[g])

    drain(query_ref.at[: 2 * tokens, :], local_sems.at[1])
    arrived(0)
    arrived(1)
    early = min(EARLY, group_size)

    @pl.loop(0, early)
    def _(g):
        head_here(g)
        softmax(g, 0)

        @pl.when((g == RELAY) & (plane >= 2))
        def _():
            for piece in pieces:
                relay(piece, 2)

    def transpose_keys(blocks):
        for j in blocks:
            key_t_ref[:, j * length : (j + 1) * length] = pair_ref[rows_of(places_of[j], length), :width].T

    transpose_keys(range(PLANE))
    arrived(2)

    @pl.loop(0, early)
    def _(g):
        softmax(g, 1)
        join(g)

    @pl.loop(early, group_size)
    def _(g):
        head_here(g)
        softmax(g, 0)
        softmax(g, 1)
        join(g)

    def dq_copies(g):
        columns = columns_of(g, width)
        landing = pl.ds(pl.multiple_of((head * group_size + g) * width, width), width)
        local = pltpu.make_async_copy(dq_ref.at[rows_here, columns], dq_out.at[:, landing], dq_sems.at[0])
        return [local] + [
            pltpu.make_async_remote_copy(
                src_ref=dq_ref.at[rows_of(peer, tokens), columns],
                dst_ref=dq_out.at[:, landing],
                send_sem=dq_sems.at[1],
                recv_sem=dq_sems.at[2],
                device_id={"head": peer},
                device_id_type=MESH,
            )
            for peer in peers
        ]

    def query_gradients():
        transpose_keys(range(PLANE, SPAN + 1))
        together = 2 - group_size % 2

        @pl.loop(0, group_size // together)
        def _(i):
            several = [i * together + k for k in range(together)]
            totals = []
            for g in several:
                places_g = columns_of(g, length)
                dq_t = jnp.zeros((width, length), jnp.float32)
                for group, here in enumerate((slice(0, half), slice(half, window))):
                    part = jnp.dot(key_t_ref[:, here], slope_ref[here, places_g], preferred_element_type=jnp.float32)
                    dq_t = dq_t + part * factor_ref[group, :1, places_g]
                totals.append(dq_t)
            for g, dq_t in zip(several, totals):
                dq_ref[:, columns_of(g, width)] = dq_t.T.astype(jnp.bfloat16)
            for g in several:
                for copy in dq_copies(g):
                    copy.start()

    back = peers + [head]

    def level_rows(level, position, piece):
        start = ((2 - level) * PLANE + position) * length + piece_start(back, piece)
        return pl.ds(pl.multiple_of(start, rows_each), rows_each)

    def slab(piece):
        return pl.ds(pl.multiple_of(piece_start(back, piece), rows_each), rows_each)

    def sum_copy(piece, kind, level):
        here = slab(piece)
        source, target, place = (
            (lambda: part_ref.at[level_rows(level, diagonal, piece), :], lambda: near_buf.at[level, 0, here], {"ctx": base + near}),
            (lambda: part_ref.at[level_rows(level, near, piece), :], lambda: near_buf.at[level, 1, here], {"ctx": base + near}),
            (lambda: far_sum.at[level, here], lambda: far_buf.at[level, here], {"ctx": base + far}),
            (lambda: down_src.at[level - 1, here], lambda: down_buf.at[level - 1, here], {"ctx": down}),
        )[kind]
        return pltpu.make_async_remote_copy(
            src_ref=source(),
            dst_ref=target(),
            send_sem=r_send.at[kind, level],
            recv_sem=r_recv.at[piece, kind, level],
            device_id=place,
            device_id_type=MESH,
        )

    def out_of(kind, level):
        if level == 1:
            return True
        return ((low, not_low), (even, not_even), (low, not_low))[kind][0 if level == 2 else 1]

    def into(kind, level):
        if level == 1:
            return True
        return ((low, not_low), (not_even, even), (not_low, low))[kind][0 if level == 2 else 1]

    def final_copies(piece):
        copies = []
        for array, target in enumerate((dk_out, dv_out)):
            source = final.at[slab(piece), lanes_of[array]]
            cols = rows_of(head, width)
            owner = piece // cut
            target = target.at[piece % cut * rows_each : (piece % cut + 1) * rows_each, :]
            if owner == len(peers):
                copies.append(pltpu.make_async_copy(source, target.at[:, cols], f_sems.at[0]))
            else:
                copies.append(
                    pltpu.make_async_remote_copy(
                        src_ref=source,
                        dst_ref=target.at[:, cols],
                        send_sem=f_sems.at[1],
                        recv_sem=f_sems.at[2],
                        device_id={"head": peers[owner]},
                        device_id_type=MESH,
                    )
                )
        return copies

    def slopes(here):
        for g in range(group_size):
            places_g = slice(g * length, (g + 1) * length)
            slope_ref[here, places_g] = (
                weight_ref[here, places_g].astype(jnp.float32)
                * (product_ref[here, places_g] - dot_ref[:1, places_g])
            ).astype(jnp.bfloat16)

    def sums(here, there, group):
        part_ref[there, :width] = (
            jnp.dot(slope_ref[here, :], query_rows[group], preferred_element_type=jnp.float32) * scaling
        ).astype(jnp.bfloat16)
        part_ref[there, width:] = jnp.dot(
            weight_ref[here, :], grad_rows[group], preferred_element_type=jnp.float32
        ).astype(jnp.bfloat16)

    def start_sums(kind, level):
        def body():
            for piece in pieces:
                sum_copy(piece, kind, level).start()
        only(out_of(kind, level), body)

    def send_far(level):
        for piece in pieces:
            here = slab(piece)
            sum_copy(piece, 0, level).wait_recv()
            far_sum[level, here] = (
                part_ref[level_rows(level, far, piece), :].astype(jnp.float32)
                + near_buf[level, 0, here].astype(jnp.float32)
            ).astype(jnp.bfloat16)
            sum_copy(piece, 2, level).start()

    def to_far(level):
        only(into(0, level), lambda: send_far(level))

    def compute(level):
        if level == 1:
            for several in ((diagonal, near), (far, slot)):
                for spot in several:
                    here = rows_of(spot, length)
                    slopes(here)
                    sums(here, rows_of(PLANE + spot, length), 0)
                if several[0] is diagonal:
                    for kind in (0, 1):
                        start_sums(kind, 1)
        elif level == 2:
            @pl.loop(0, PLANE - slot)
            def _(i):
                spot = slot + i
                turned = jnp.where(i == 0, diagonal, jnp.where(i == 1, far, slot + i - PLANE // 2))
                spot = jnp.where(low, turned, spot)
                here = rows_of(PLANE - slot + spot, length)
                slopes(here)
                sums(here, rows_of(spot, length), 1)

                @pl.when(low & (i == 0))
                def _():
                    for piece in pieces:
                        sum_copy(piece, 0, 2).start()

                @pl.when(low & (i == 1))
                def _():
                    send_far(2)

            start_sums(1, 2)
        else:
            @pl.loop(0, slot + 1)
            def _(i):
                here = rows_of(SPAN - slot + i, length)
                slopes(here)
                sums(here, rows_of(2 * PLANE + i, length), 1)

            for kind in (0, 1):
                start_sums(kind, 0)

    def collect(level):
        for piece in pieces:
            here = slab(piece)
            own_sum[level, here] = part_ref[level_rows(level, slot, piece), :].astype(jnp.float32)

            def add_near():
                sum_copy(piece, 1, level).wait_recv()
                own_sum[level, here] += near_buf[level, 1, here].astype(jnp.float32)
            only(into(1, level), add_near)

            def add_far():
                sum_copy(piece, 2, level).wait_recv()
                own_sum[level, here] += far_buf[level, here].astype(jnp.float32)
            only(into(2, level), add_far)

            if level < 2:
                @pl.when(plane < last)
                def _():
                    sum_copy(piece, 3, level + 1).wait_recv()
                    own_sum[level, here] += down_buf[level, here].astype(jnp.float32)

            if level > 0:
                down_src[level - 1, here] = own_sum[level, here].astype(jnp.bfloat16)
                sum_copy(piece, 3, level).start()
            else:
                final[here] = own_sum[level, here].astype(jnp.bfloat16)
                for copy in final_copies(piece):
                    copy.start()

    def on_level(level, body):
        only(True if level == 0 else plane >= level, lambda: body(level))

    @pl.when(plane < 1)
    def _():
        slope_ref[:half, :] = jnp.zeros((half, slope_ref.shape[1]), slope_ref.dtype)

    @pl.when(plane < 2)
    def _():
        @pl.loop(0, PLANE - slot)
        def _(i):
            slope_ref[rows_of(PLANE + i, length), :] = jnp.zeros((length, slope_ref.shape[1]), slope_ref.dtype)

    on_level(2, compute)
    on_level(1, compute)
    on_level(1, to_far)
    on_level(0, compute)
    on_level(2, collect)
    on_level(0, to_far)
    query_gradients()
    on_level(1, collect)
    on_level(0, collect)

    for level in range(3):
        @pl.when(plane >= level)
        def _():
            for kind in range(4):
                def wait_forward():
                    drain(whole_block, c_send.at[kind, level])
                if kind == 0:
                    if level < 2:
                        only(plane < last, wait_forward)
                elif kind == 3:
                    only(receives(1, level), wait_forward)
                else:
                    only(sends(kind, level), wait_forward)

            for kind in range(4):
                def wait_back():
                    drain(whole_block, r_send.at[kind, level])
                if kind == 3:
                    if level:
                        wait_back()
                elif kind == 2:
                    only(into(0, level), wait_back)
                else:
                    only(out_of(kind, level), wait_back)

    drain(pair_ref.at[:others, :], x_send)
    drain(weight_ref.at[: 2 * others, : group_size * width], q_send)
    for index, count in enumerate((tokens, others, others)):
        drain(query_ref.at[:count, :], dq_sems.at[index])
        drain(pair_ref.at[:count, :], f_sems.at[index])


def attention(queries, output_cotangent, keys, values, docs):
    heads = lax.axis_size("head")
    tokens, query_width = queries.shape
    length = tokens * heads
    width = keys.shape[1] // heads
    group_size = query_width // heads // width
    window = (SPAN + 1) * length
    anywhere = pl.BlockSpec(memory_space=pl.ANY)
    dma = pltpu.SemaphoreType.DMA
    rows = (length, query_width // heads)
    block = (length, 2 * width)
    bf16, f32 = jnp.bfloat16, jnp.float32
    narrow = jax.ShapeDtypeStruct((tokens, width * heads), bf16)
    return pl.pallas_call(
        functools.partial(attention_kernel, scaling=width ** (-0.5)),
        out_shape=(jax.ShapeDtypeStruct((tokens, query_width), bf16), narrow, narrow),
        in_specs=[anywhere] * 5,
        out_specs=(anywhere,) * 3,
        scratch_shapes=[
            pltpu.VMEM(rows, bf16),
            pltpu.VMEM(rows, bf16),
            pltpu.VMEM((SLOTS * length, 2 * width), bf16),
            pltpu.VMEM(docs.shape, docs.dtype),
            pltpu.VMEM((window, length), f32),
            pltpu.VMEM((width, window), bf16),
            pltpu.VMEM((window - PLANE * length, length), f32),
            pltpu.VMEM((window, group_size * length), f32),
            pltpu.VMEM((window, group_size * length), bf16),
            pltpu.VMEM((window, group_size * length), bf16),
            pltpu.VMEM((2, group_size * length, width), bf16),
            pltpu.VMEM((2, group_size * length, width), bf16),
            pltpu.VMEM(rows, bf16),
            pltpu.VMEM((group_size, 2, 3, 8, length), f32),
            pltpu.VMEM((8, group_size * length), f32),
            pltpu.VMEM((2, 8, group_size * length), f32),
            pltpu.VMEM((SLOTS * length, 2 * width), bf16),
            pltpu.VMEM((3, 2) + block, bf16),
            pltpu.VMEM((3,) + block, f32),
            pltpu.VMEM((3,) + block, bf16),
            pltpu.VMEM((3,) + block, bf16),
            pltpu.VMEM((2,) + block, bf16),
            pltpu.VMEM((2,) + block, bf16),
            pltpu.VMEM(block, bf16),
            dma((3,)), dma, dma((heads - 1,)), dma, dma((group_size,)),
            dma((4, 3)), dma((heads * pieces_of(tokens), 2, 3)), dma((2, 3)),
            dma((3,)), dma((4, 3)), dma((heads * pieces_of(tokens), 4, 3)), dma((3,)),
        ],
        compiler_params=pltpu.CompilerParams(
            collective_id=0, has_side_effects=True, vmem_limit_bytes=VMEM_LIMIT
        ),
    )(queries, output_cotangent, keys, values, docs)


def settle_kernel(dq_ref, dk_ref, dv_ref, dq_out, dk_out, dv_out, sems):
    copies = [
        pltpu.make_async_copy(source, target, sems.at[index])
        for index, (source, target) in enumerate(((dq_ref, dq_out), (dk_ref, dk_out), (dv_ref, dv_out)))
    ]
    for copy in copies:
        copy.start()
    for copy in copies:
        copy.wait()


def settle(*arrays):
    return pl.pallas_call(
        settle_kernel,
        out_shape=tuple(jax.ShapeDtypeStruct(array.shape, array.dtype) for array in arrays),
        in_specs=[pl.BlockSpec(memory_space=pltpu.VMEM)] * 3,
        out_specs=(pl.BlockSpec(memory_space=pl.ANY),) * 3,
        scratch_shapes=[pltpu.SemaphoreType.DMA((3,))],
    )(*arrays)


def on_device(queries, keys, values, output_cotangent, doc_ids):
    docs = doc_ids.reshape(-1, keys.shape[1] // lax.axis_size("head"))
    return settle(*attention(queries, output_cotangent, keys, values, docs))


def solution(mesh):
    rows = P(("ctx", "head"), None)
    return jax.shard_map(
        on_device,
        mesh=mesh,
        in_specs=(rows, rows, rows, rows, P()),
        out_specs=(rows, rows, rows),
        check_vma=False,
    )
```
